256 devices in a mesh: seq: 32 (over z, y), head: 8 (over x, core).
Axes of the slice: x: 4, y: 4, z: 8, core: 2. Of those that a mesh axis runs over, the one named last changes fastest.
Arguments:
- query: bfloat16 [16384, 4096], P('seq', 'head'), may hold values from -9 to 9
- keys: bfloat16 [16384, 1024], P('seq', 'head'), may hold values from -9 to 9
- values: bfloat16 [16384, 1024], P('seq', 'head'), may hold values from -6 to 6
- grad_out: bfloat16 [16384, 4096], P('seq', 'head'), may hold values from -6 to 6
- w_query: bfloat16 [4096, 4096], P(None, 'head'), may hold values from -0.5 to 0.5
- w_key: bfloat16 [4096, 1024], P(None, 'head'), may hold values from -0.5 to 0.5
- w_value: bfloat16 [4096, 1024], P(None, 'head'), may hold values from -0.5 to 0.5
- rand_owner: int32 [256, 3], replicated, may hold values from 0 to 31, all different within a row; in each aligned block of 8 rows (0 to 7, 8 to 15, ...) at most 2 rows name the same one
- rand_block: int32 [256, 3], replicated, may hold values from 0 to 7
Outputs:
- grad_input: bfloat16 [16384, 4096], P(('seq', 'head'))
The draws below stay inside these ranges and needn't reach their ends.
Inputs may be any that keep to these rules, and one draw needn't show every extreme that they name: `rand_owner`: the 3 entries of a row differ; among the rows of one run of 8 query blocks (aligned blocks of rows) no value appears more than 2 times.
All inputs are finite; a program needn't handle non-finite values.
Results may differ from the reference program's by a relative error of at most 0.014.
Values may be sent and summed in bfloat16 or wider, within the bound.
A program may use at most 128 MiB of HBM per device.

```python
import math
import jax
import jax.numpy as jnp
import numpy as np
from jax import lax

D = 4096
HEADS = 32
KV_HEADS = 8
HEAD_DIM = 128
BLOCK = 64
GLOBAL = 2
RANDOM = 3
TOKENS = 16384
QB_DEV = 8
QBLOCKS = 256
Q_DEV = 4
KV_DEV = 1
HEAD_GROUPS = 8
CAP = 2
LIST = 8
N_SEQ = 32


def drawn_rows(key):
    base = jax.random.fold_in(key, 4242)
    streams = jax.random.split(base, 5)
    group_size = HEADS // KV_HEADS
    query_rows = jnp.clip(jax.random.normal(streams[3], (TOKENS, KV_HEADS, group_size, HEAD_DIM), jnp.float32), -4.0, 4.0)
    key_rows = jnp.clip(jax.random.normal(streams[4], (TOKENS, KV_HEADS, HEAD_DIM), jnp.float32), -4.0, 4.0)
    return (query_rows.reshape(TOKENS, HEADS * HEAD_DIM), key_rows.reshape(TOKENS, KV_HEADS * HEAD_DIM))


def draw_query(key, part):
    query_rows, key_rows = drawn_rows(key)
    return query_rows.astype(jnp.bfloat16)


def draw_keys(key, part):
    query_rows, key_rows = drawn_rows(key)
    return key_rows.astype(jnp.bfloat16)


def place_ends(entries, stream_key, smallest, high):
    spot = [jax.random.randint(jax.random.fold_in(stream_key, axis), (), 0, length) for axis, length in enumerate(entries.shape)]
    longest = entries.shape.index(max(entries.shape))
    next_to = spot[:longest] + [(spot[longest] + 1) % entries.shape[longest]] + spot[longest + 1:]
    return entries.at[tuple(spot)].set(smallest).at[tuple(next_to)].set(high)


def block_levels(key, dims, cuts, low, top_value):
    loudness = 1.0
    for axis_at, shards_of in cuts:
        draws = jax.random.uniform(jax.random.fold_in(jax.random.fold_in(key, 6), axis_at), (shards_of,), jnp.float32, low / len(cuts), top_value / len(cuts))
        loudness = loudness * jnp.repeat(jnp.exp(draws), dims[axis_at] // shards_of).reshape((-1,) + (1,) * (len(dims) - 1 - axis_at))
    return loudness


def routed_block(stream_key, own, number, rows, number_of, top, reach, slope):
    sequence = jax.random.permutation(stream_key, number_of)
    packed, common = shares(number_of, rows * top, reach, slope, True), shares(number_of, rows * top, reach, slope, False)
    places = jnp.arange(number_of)

    def named(tallies, turn):
        used = int((tallies > 0).sum())
        fixed = max(1, used // 4)
        shifted = fixed + (places - fixed + turn * (used - fixed)) % max(1, number_of - fixed)
        return jnp.zeros((number_of,), jnp.int32).at[sequence[jnp.where(places < fixed, places, shifted)]].set(jnp.asarray(tallies, jnp.int32))

    tallies = jnp.where(number % 4 == 0, named(packed, number // 4), named(common, number - number // 4 - 1))
    mixed = jax.random.permutation(jax.random.fold_in(own, 3), number_of)
    source_of, taker = mixed[0:number_of // 2 * 2:2], mixed[1:number_of // 2 * 2:2]
    slack = jnp.minimum(tallies[source_of] - 1, reach - tallies[taker]) // 2
    slack = jnp.where((source_of == sequence[0]) | (taker == sequence[0]) | (tallies[taker] == 0), 0, jnp.maximum(slack, 0))
    shifted = jax.random.randint(jax.random.fold_in(own, 4), (number_of // 2,), 0, 1 << 20) % (slack + 1)
    tallies = tallies.at[source_of].add(-shifted).at[taker].add(shifted)
    items = jnp.searchsorted(jnp.cumsum(tallies), jnp.arange(rows * top), side="right").astype(jnp.int32)
    grid = items.reshape(top, rows).T
    grid = grid[jax.random.permutation(jax.random.fold_in(own, 1), rows)]
    turn = jax.random.randint(jax.random.fold_in(own, 2), (rows, 1), 0, top)
    return jnp.take_along_axis(grid, (jnp.arange(top)[None, :] + turn) % top, axis=1)


def shares(count, total, limit, slope, full):
    loads = [(1 << 20) // math.isqrt(grade ** slope) + 1 for grade in range(1, count + 1)]
    largest = limit if full else min(limit, max(-(-total // count), total * loads[0] // sum(loads)))
    least = 1 if total - largest >= count - 1 else 0
    counts, spare = [largest] + [least] * (count - 1), total - largest - least * (count - 1)
    while spare > 0:
        candidates = [i for i in range(1, count) if counts[i] < largest] or [i for i in range(1, count) if counts[i] < limit]
        mass, remaining = sum([loads[i] for i in candidates]), spare
        for i in candidates:
            extra = min(limit - counts[i], max(1, remaining * loads[i] // mass), spare)
            counts[i] = counts[i] + extra
            spare = spare - extra
    return np.array(counts)


def gaussian(own_key, dims, scale, bound, pieces=(), kind=jnp.bfloat16):
    result = jax.random.normal(own_key, dims, jnp.float32) * scale
    if len(pieces) > 0:
        result = block_levels(own_key, dims, pieces, -0.22, 0.18) * result
    return jnp.clip(result, min=-bound, max=bound).astype(kind)


def setup_inputs(seed: int = 0) -> dict:
    arg_keys = jax.random.split(jax.random.key(seed), 10)
    query = draw_query(jax.random.fold_in(arg_keys[9], 71), 0)
    keys = draw_keys(jax.random.fold_in(arg_keys[9], 71), 0)
    values = gaussian(arg_keys[2], (TOKENS, KV_HEADS * HEAD_DIM), 1.0, 6.0, ((0, 32), (1, 8)))
    grad_out = gaussian(arg_keys[3], (TOKENS, HEADS * HEAD_DIM), 1.0, 6.0, ((0, 32), (1, 8)))
    w_query = gaussian(arg_keys[4], (D, HEADS * HEAD_DIM), HEAD_DIM ** -0.5, 0.5, ((1, 8),))
    w_key = gaussian(arg_keys[5], (D, KV_HEADS * HEAD_DIM), HEAD_DIM ** -0.5, 0.5, ((1, 8),))
    w_value = gaussian(arg_keys[6], (D, KV_HEADS * HEAD_DIM), HEAD_DIM ** -0.5, 0.5, ((1, 8),))
    rand_owner_keys = jax.random.split(jax.random.fold_in(arg_keys[7], 1), QBLOCKS // QB_DEV)
    rand_owner_turns = jax.random.permutation(jax.random.fold_in(arg_keys[7], 3), QBLOCKS // QB_DEV)
    rand_owner = jax.vmap(lambda own, number: routed_block(jax.random.fold_in(arg_keys[7], 2), own, number, QB_DEV, N_SEQ, RANDOM, CAP, 2))(rand_owner_keys, rand_owner_turns).reshape((QBLOCKS, RANDOM))
    rand_block = place_ends(jax.random.randint(arg_keys[8], (QBLOCKS, RANDOM), 0, QB_DEV), jax.random.fold_in(arg_keys[8], 1), 0, QB_DEV - 1).astype(jnp.int32)
    return dict(query=query, keys=keys, values=values, grad_out=grad_out, w_query=w_query, w_key=w_key, w_value=w_value, rand_owner=rand_owner, rand_block=rand_block)


def to_half(value):
    return lax.optimization_barrier(value.astype(jnp.bfloat16))


def key_lists(rand_owner, rand_block):
    block_ids = jnp.arange(QBLOCKS, dtype=jnp.int32)
    window = jnp.stack([block_ids - 1, block_ids, block_ids + 1], axis=1)
    usable = (window >= 0) & (window < QBLOCKS)
    window = jnp.clip(window, 0, QBLOCKS - 1).astype(jnp.int32)
    global_ids = jnp.broadcast_to(jnp.arange(GLOBAL, dtype=jnp.int32)[None, :], (QBLOCKS, GLOBAL))
    random_ids = (rand_owner * QB_DEV + rand_block).astype(jnp.int32)
    listed = jnp.concatenate([window, global_ids, random_ids], axis=1)
    usable = jnp.concatenate([usable, jnp.ones((QBLOCKS, GLOBAL + RANDOM), dtype=bool)], axis=1)
    return listed, usable


def head_grads(q_head, k_head, v_head, do_head, listed, usable):
    scale = HEAD_DIM ** -0.5
    key_rows = k_head.reshape(QBLOCKS, BLOCK, HEAD_DIM)[listed].reshape(QBLOCKS, LIST * BLOCK, HEAD_DIM).astype(jnp.float32)
    value_rows = v_head.reshape(QBLOCKS, BLOCK, HEAD_DIM)[listed].reshape(QBLOCKS, LIST * BLOCK, HEAD_DIM).astype(jnp.float32)
    q_full = q_head.astype(jnp.float32)
    do_full = do_head.astype(jnp.float32)
    scores = jnp.einsum("nigd,njd->ngij", q_full, key_rows) * scale
    mask = jnp.repeat(usable, BLOCK, axis=1)[:, None, None, :]
    scores = jnp.where(mask, scores, -1e30)
    row_max = jnp.max(scores, axis=-1, keepdims=True)
    powers = jnp.exp(scores - row_max)
    attn_weights = powers / jnp.sum(powers, axis=-1, keepdims=True)
    weights_half = to_half(attn_weights).astype(jnp.float32)
    attn_out = jnp.einsum("ngij,njd->nigd", weights_half, value_rows)
    delta = jnp.sum(do_full * attn_out, axis=-1)
    dprob = jnp.einsum("nigd,njd->ngij", do_full, value_rows)
    dscore = attn_weights * (dprob - jnp.transpose(delta, (0, 2, 1))[..., None])
    dscore_half = to_half(dscore).astype(jnp.float32)
    grad_query = (jnp.einsum("ngij,njd->nigd", dscore_half, key_rows) * scale).astype(jnp.bfloat16)
    key_part = jnp.einsum("ngij,nigd->njd", dscore_half, q_full) * scale
    value_part = jnp.einsum("ngij,nigd->njd", weights_half, do_full)
    partial_value = jnp.concatenate([key_part, value_part], axis=-1).reshape(QBLOCKS, LIST, BLOCK, 2 * HEAD_DIM)
    grad_kv = jnp.zeros((QBLOCKS, BLOCK, 2 * HEAD_DIM), jnp.float32)
    grad_kv = grad_kv.at[listed[:, :3]].add(partial_value[:, :3])
    runs = jnp.sum(partial_value[:, 3:3 + GLOBAL].reshape(N_SEQ, QB_DEV, GLOBAL, BLOCK, 2 * HEAD_DIM), axis=1)
    runs = jnp.sum(to_half(runs).astype(jnp.float32), axis=0)
    grad_kv = grad_kv.at[:GLOBAL].add(runs)
    random_half = to_half(partial_value[:, 3 + GLOBAL:]).astype(jnp.float32)
    grad_kv = grad_kv.at[listed[:, 3 + GLOBAL:]].add(random_half)
    return grad_query, grad_kv.astype(jnp.bfloat16)


def reference(query, keys, values, grad_out, w_query, w_key, w_value, rand_owner, rand_block):
    listed, usable = key_lists(rand_owner, rand_block)
    group_size = HEADS // KV_HEADS
    q_heads = query.reshape(QBLOCKS, BLOCK, KV_HEADS, group_size, HEAD_DIM).transpose(2, 0, 1, 3, 4)
    do_heads = grad_out.reshape(QBLOCKS, BLOCK, KV_HEADS, group_size, HEAD_DIM).transpose(2, 0, 1, 3, 4)
    k_heads = keys.reshape(TOKENS, KV_HEADS, HEAD_DIM).transpose(1, 0, 2)
    v_heads = values.reshape(TOKENS, KV_HEADS, HEAD_DIM).transpose(1, 0, 2)

    def one_head(items):
        return head_grads(items[0], items[1], items[2], items[3], listed, usable)

    grad_query, grad_kv = lax.map(one_head, (q_heads, k_heads, v_heads, do_heads))
    grad_query = grad_query.transpose(1, 2, 0, 3, 4).reshape(TOKENS, HEADS * HEAD_DIM)
    grad_keys = grad_kv[..., :HEAD_DIM].transpose(1, 2, 0, 3).reshape(TOKENS, KV_HEADS * HEAD_DIM)
    grad_values = grad_kv[..., HEAD_DIM:].transpose(1, 2, 0, 3).reshape(TOKENS, KV_HEADS * HEAD_DIM)
    q_width = Q_DEV * HEAD_DIM
    k_width = KV_DEV * HEAD_DIM
    dq_groups = grad_query.reshape(TOKENS, HEAD_GROUPS, q_width).transpose(1, 0, 2)
    dk_groups = grad_keys.reshape(TOKENS, HEAD_GROUPS, k_width).transpose(1, 0, 2)
    dv_groups = grad_values.reshape(TOKENS, HEAD_GROUPS, k_width).transpose(1, 0, 2)
    wq_groups = w_query.reshape(D, HEAD_GROUPS, q_width).transpose(1, 0, 2)
    wk_groups = w_key.reshape(D, HEAD_GROUPS, k_width).transpose(1, 0, 2)
    wv_groups = w_value.reshape(D, HEAD_GROUPS, k_width).transpose(1, 0, 2)

    def add_group(total, items):
        dq_rows, dk_rows, dv_rows, wq_rows, wk_rows, wv_rows = items
        term = jnp.dot(dq_rows, wq_rows.T, preferred_element_type=jnp.float32)
        term = term + jnp.dot(dk_rows, wk_rows.T, preferred_element_type=jnp.float32)
        term = term + jnp.dot(dv_rows, wv_rows.T, preferred_element_type=jnp.float32)
        return total + to_half(term).astype(jnp.float32), None

    start = jnp.zeros((TOKENS, D), jnp.float32)
    total, unused = lax.scan(add_group, start, (dq_groups, dk_groups, dv_groups, wq_groups, wk_groups, wv_groups))
    return total.astype(jnp.bfloat16)
```

```python
import functools

import jax
import jax.numpy as jnp
from jax import lax
from jax.experimental import pallas as pl
from jax.experimental.pallas import tpu as pltpu
from jax.sharding import PartitionSpec as P

BLOCK = 64
HD = 128
NZ = 8
NY = 4
NX = 4
RUN = 8
ROWS = RUN * BLOCK
GROUP = 4
D = 4096
SLOT0 = NZ * RUN
EXTRA0 = SLOT0 + 3 * 2 * NZ
TABLE = EXTRA0 + 4
REL = (0, 1, 3, 2)
MESH = pl.DeviceIdType.MESH
SCALE = HD ** (-0.5)
VM = pltpu.VMEM


def vmem():
    return pl.BlockSpec(memory_space=pltpu.VMEM)


def smem():
    return pl.BlockSpec(memory_space=pltpu.SMEM)


def seq_place():
    s = lax.axis_index("seq")
    return s, lax.div(s, NY), lax.rem(s, NY)


def rows_of(start, size):
    return pl.ds(pl.multiple_of(start, BLOCK), size)


def prep_kernel(owner_ref, block_ref, picks_ref, list_ref, slot_ref, count_ref):
    s, z, y = seq_place()
    for i in range(4):
        for n in range(32):
            count_ref[i * 32 + n] = 0
        for n in range(16):
            picks_ref[i * 16 + n] = -1
            picks_ref[72 + i * 16 + n] = 0

    for i in range(4):
        row0 = (z * NY + lax.rem(y + REL[i], NY)) * RUN

        def per_row(b, carry):
            for j in range(3):
                owner = owner_ref[row0 + b, j]
                pick = block_ref[row0 + b, j]
                place = count_ref[i * 32 + owner]
                count_ref[i * 32 + owner] = place + 1
                zo = lax.div(owner, NY)
                yo = lax.rem(owner, NY)
                at = zo * 2 + place
                slot = jnp.where(yo == y, i * 16 + at, 64 + j)
                picks_ref[slot] = pick
                picks_ref[72 + slot] = pick
                if i == 0:
                    rel = lax.rem(yo - y + NY, NY)
                    reg = jnp.where(rel == 3, 2, jnp.where(rel == 2, 3, rel))
                    list_ref[b * 8 + 5 + j] = jnp.where(
                        reg == 0, zo * RUN + pick, SLOT0 + (reg - 1) * 16 + at
                    )
                    slot_ref[b * 3 + j] = reg * 16 + at
            if i == 0:
                list_ref[b * 8] = jnp.where(b == 0, EXTRA0, z * RUN + b - 1)
                list_ref[b * 8 + 1] = z * RUN + b
                list_ref[b * 8 + 2] = jnp.where(b == RUN - 1, EXTRA0 + 1, z * RUN + b + 1)
                list_ref[b * 8 + 3] = EXTRA0 + 2
                list_ref[b * 8 + 4] = EXTRA0 + 3
            return carry

        lax.fori_loop(0, RUN, per_row, 0)


def neighbours(z, y):
    return (
        lax.rem(z + 1, NZ) * NY + y,
        lax.rem(z + NZ - 1, NZ) * NY + y,
        z * NY + lax.rem(y + 1, NY),
        z * NY + lax.rem(y + 3, NY),
        z * NY + lax.rem(y + 2, NY),
    )


def greet(peers, axis):
    barrier = pltpu.get_barrier_semaphore()
    for peer in peers:
        pl.semaphore_signal(barrier, inc=1, device_id={axis: peer}, device_id_type=MESH)
    pl.semaphore_wait(barrier, len(peers))


def send(src, dst, ssem, rsem, axis, peer):
    return pltpu.make_async_remote_copy(
        src_ref=src,
        dst_ref=dst,
        send_sem=ssem,
        recv_sem=rsem,
        device_id={axis: peer},
        device_id_type=MESH,
    )


def fetch_kernel(
    picks_ref, k_ref, v_ref, tab, stage, sendbuf, zs, zr, ys, yr, hs, hr, gs, gr
):
    s, z, y = seq_place()
    zu, zd, yp, ym, y2 = neighbours(z, y)
    ypeers = (yp, ym, y2)
    theirs = (1, 0, 2)
    own = (k_ref, v_ref)
    greet((zu, zd, yp, ym, y2), "seq")

    def ring(up, t, kv):
        chunk = lax.rem(z + (NZ - t if up else t), NZ)
        where = tab.at[kv, rows_of(chunk * ROWS, ROWS)]
        i = 0 if up else 1
        return send(
            own[kv] if t == 0 else where, where, zs.at[i, t, kv], zr.at[i, t, kv],
            "seq", zu if up else zd,
        )

    def landed(up, t, kv):
        chunk = lax.rem(z + (NZ - 1 - t if up else 1 + t), NZ)
        where = tab.at[kv, rows_of(chunk * ROWS, ROWS)]
        i = 0 if up else 1
        return send(where, where, zs.at[i, t, kv], zr.at[i, t, kv], "seq", zu if up else zd)

    def slot_copy(p, chunk):
        at = rows_of((SLOT0 + theirs[p] * 16 + chunk * 2) * BLOCK, 2 * BLOCK)
        return send(
            sendbuf.at[p, chunk], tab.at[:, at, :], ys.at[p, chunk], yr.at[theirs[p], chunk],
            "seq", ypeers[p],
        )

    def global_copy(p):
        return send(
            tab.at[:, pl.ds(0, 2 * BLOCK), :],
            tab.at[:, pl.ds((EXTRA0 + 2) * BLOCK, 2 * BLOCK), :],
            gs.at[p], gr, "seq", ypeers[p],
        )

    def halo_copy(p):
        if p == 0:
            chunk = lax.rem(z + NZ - lax.div(y, 3), NZ)
            row = chunk * ROWS + (RUN - 1) * BLOCK
        else:
            chunk = lax.rem(z + lax.div(3 - y, 3), NZ)
            row = chunk * ROWS
        at = pl.ds((EXTRA0 + p) * BLOCK, BLOCK)
        return send(
            tab.at[:, rows_of(row, BLOCK), :], tab.at[:, at, :], hs.at[p], hr.at[p],
            "seq", ypeers[p],
        )

    def spread(chunk):
        for kv in range(2):
            stage[kv] = tab[kv, rows_of(chunk * ROWS, ROWS), :].reshape(RUN, BLOCK, HD)
        for p in range(3):
            for k in range(2):
                pick = picks_ref[72 + (p + 1) * 16 + chunk * 2 + k]
                for kv in range(2):
                    sendbuf[p, chunk, kv, k * BLOCK : (k + 1) * BLOCK, :] = stage[kv, pick]
        for p in range(3):
            slot_copy(p, chunk).start()

        @pl.when(jnp.logical_and(chunk == 0, y == 0))
        def _():
            for p in range(3):
                global_copy(p).start()

    for kv in range(2):
        ring(True, 0, kv).start()
        ring(False, 0, kv).start()
    for kv in range(2):
        tab[kv, rows_of(z * ROWS, ROWS), :] = own[kv][...]
    spread(z)
    for t in range(4):
        for kv in range(2):
            for up in (True, False):
                if t == 3 and kv != (0 if up else 1):
                    continue
                landed(up, t, kv).wait_recv()
                if t < 2 or (t == 2 and kv == (0 if up else 1)):
                    ring(up, t + 1, kv).start()
        if t == 0:
            halo_copy(0).start()
            halo_copy(1).start()
        spread(lax.rem(z + NZ - 1 - t, NZ))
        if t < 3:
            spread(lax.rem(z + 1 + t, NZ))

    for c in range(NZ):
        for p in range(3):
            slot_copy(p, c).wait_recv()
    for p in range(2):
        halo_copy(p).wait_recv()

    @pl.when(y == 0)
    def _():
        for kv in range(2):
            tab[kv, (EXTRA0 + 2) * BLOCK : (EXTRA0 + 4) * BLOCK, :] = tab[kv, 0 : 2 * BLOCK, :]
        for p in range(3):
            global_copy(p).wait_send()

    @pl.when(y != 0)
    def _():
        global_copy(0).wait_recv()

    for t in range(4):
        for kv in range(2):
            for up in (True, False):
                if t == 3 and kv != (0 if up else 1):
                    continue
                ring(up, t, kv).wait_send()
    for c in range(NZ):
        for p in range(3):
            slot_copy(p, c).wait_send()
    for p in range(2):
        halo_copy(p).wait_send()


NT = (((1,), (1,)), ((), ()))
NN = (((1,), (0,)), ((), ()))
TN = (((0,), (0,)), ((), ()))


def dot(a, b, dims):
    return lax.dot_general(a, b, dims, preferred_element_type=jnp.float32)


def attend_kernel(
    list_ref, slot_ref, q_ref, do_ref, tab, dq_ref, part, wloc, halo, glob, kl, vl, wacc, gacc
):
    b = pl.program_id(0)
    s = lax.axis_index("seq")

    @pl.when(b == 0)
    def _():
        wacc[...] = jnp.zeros_like(wacc)
        gacc[...] = jnp.zeros_like(gacc)

    for j in range(8):
        at = rows_of(list_ref[b * 8 + j] * BLOCK, BLOCK)
        kl[j * BLOCK : (j + 1) * BLOCK, :] = tab[0, at, :]
        vl[j * BLOCK : (j + 1) * BLOCK, :] = tab[1, at, :]
    q4 = jnp.concatenate([q_ref[:, g * HD : (g + 1) * HD] for g in range(GROUP)], axis=0)
    d4 = jnp.concatenate([do_ref[:, g * HD : (g + 1) * HD] for g in range(GROUP)], axis=0)
    keys = kl[...]
    vals = vl[...]
    scores = dot(keys, q4, NT) * SCALE
    no_left = jnp.logical_and(s == 0, b == 0)
    no_right = jnp.logical_and(s == NZ * NY - 1, b == RUN - 1)
    scores = jnp.concatenate(
        [
            jnp.where(no_left, -1e30, scores[:BLOCK]),
            scores[BLOCK : 2 * BLOCK],
            jnp.where(no_right, -1e30, scores[2 * BLOCK : 3 * BLOCK]),
            scores[3 * BLOCK :],
        ],
        axis=0,
    )
    row_max = jnp.max(scores, axis=0, keepdims=True)
    powers = jnp.exp(scores - row_max)
    weights = powers * (1.0 / jnp.sum(powers, axis=0, keepdims=True))
    weights_half = weights.astype(jnp.bfloat16)
    dprob = dot(vals, d4, NT)
    delta = jnp.sum(weights_half.astype(jnp.float32) * dprob, axis=0, keepdims=True)
    dscore_half = (weights * (dprob - delta)).astype(jnp.bfloat16)
    dq = (dot(dscore_half, keys, TN) * SCALE).astype(jnp.bfloat16)
    for g in range(GROUP):
        dq_ref[:, g * HD : (g + 1) * HD] = dq[g * BLOCK : (g + 1) * BLOCK]
    parts = (dot(dscore_half, q4, NN) * SCALE, dot(weights_half, d4, NN))
    for kv in range(2):
        grad = parts[kv]
        wacc[kv, rows_of(b * BLOCK, 3 * BLOCK), :] += grad[: 3 * BLOCK]
        gacc[kv] += grad[3 * BLOCK : 5 * BLOCK]
        for j in range(3):
            at = rows_of(slot_ref[b * 3 + j] * BLOCK, BLOCK)
            part[kv, at, :] = grad[(5 + j) * BLOCK : (6 + j) * BLOCK].astype(jnp.bfloat16)

    @pl.when(b == RUN - 1)
    def _():
        for kv in range(2):
            wloc[kv] = wacc[kv, BLOCK : BLOCK + ROWS, :]
            halo[kv, :BLOCK, :] = wacc[kv, :BLOCK, :].astype(jnp.bfloat16)
            halo[kv, BLOCK:, :] = wacc[kv, BLOCK + ROWS :, :].astype(jnp.bfloat16)
            glob[kv] = gacc[kv].astype(jnp.bfloat16)


def return_kernel(
    picks_ref, part, wloc, halo, glob, dk_ref, dv_ref,
    ybuf, hbuf, gbuf, acc, zup, zdown, zs, zr, ys, yr, hs, hr, gs, gr
):
    s, z, y = seq_place()
    zu, zd, yp, ym, y2 = neighbours(z, y)
    ypeers = (yp, ym, y2)
    theirs = (1, 0, 2)
    greet((zu, zd, yp, ym, y2), "seq")

    def slot_copy(p, chunk):
        at = rows_of(((p + 1) * 16 + chunk * 2) * BLOCK, 2 * BLOCK)
        return send(
            part.at[:, at, :], ybuf.at[theirs[p], chunk], ys.at[p, chunk],
            yr.at[theirs[p], chunk], "seq", ypeers[p],
        )

    def halo_copy(p):
        half = pl.ds(BLOCK if p == 0 else 0, BLOCK)
        return send(
            halo.at[:, half, :], hbuf.at[theirs[p]], hs.at[p], hr.at[theirs[p]],
            "seq", ypeers[p],
        )

    def global_copy(slot):
        return send(glob, gbuf.at[slot], gs, gr.at[slot], "seq", z * NY)

    order = (4, 3, -3, 2, -2, 1, -1, 0)

    halo_copy(0).start()
    halo_copy(1).start()
    for n in range(1, NY):
        @pl.when(y == n)
        def _():
            global_copy(n - 1).start()
    for off in order:
        chunk = lax.rem(z + off + NZ, NZ)
        for p in range(3):
            slot_copy(p, chunk).start()

    for p in range(2):
        halo_copy(p).wait_recv()

    @pl.when(y == 0)
    def _():
        for n in range(3):
            global_copy(n).wait_recv()

    low_chunk = lax.rem(z + NZ - lax.div(y, 3), NZ)
    high_chunk = lax.rem(z + lax.div(3 - y, 3), NZ)

    def collect(chunk):
        for p in range(3):
            slot_copy(p, chunk).wait_recv()
        picks = [
            [picks_ref[i * 16 + chunk * 2 + k] for k in range(2)] for i in range(4)
        ]

        def one(b, carry):
            for kv in range(2):
                total = jnp.zeros((BLOCK, HD), jnp.float32)
                for i in range(4):
                    for k in range(2):
                        if i == 0:
                            at = rows_of((chunk * 2 + k) * BLOCK, BLOCK)
                            piece = part[kv, at, :]
                        else:
                            piece = ybuf[i - 1, chunk, kv, k * BLOCK : (k + 1) * BLOCK, :]
                        total = total + jnp.where(
                            picks[i][k] == b, piece.astype(jnp.float32), 0.0
                        )
                acc[kv, rows_of(b * BLOCK, BLOCK), :] = total
            return carry

        lax.fori_loop(0, RUN, one, 0)
        last = pl.ds((RUN - 1) * BLOCK, BLOCK)
        first = pl.ds(0, BLOCK)

        @pl.when(chunk == low_chunk)
        def _():
            for kv in range(2):
                acc[kv, last, :] += hbuf[0, kv].astype(jnp.float32)

        @pl.when(chunk == high_chunk)
        def _():
            for kv in range(2):
                acc[kv, first, :] += hbuf[1, kv].astype(jnp.float32)

        @pl.when(jnp.logical_and(chunk == 0, y == 0))
        def _():
            for kv in range(2):
                total = glob[kv].astype(jnp.float32)
                for n in range(3):
                    total = total + gbuf[n, kv].astype(jnp.float32)
                acc[kv, 0 : 2 * BLOCK, :] += total

    bufs = (zup, zdown)
    zpeer = (zu, zd)

    def ring(i, t, kv):
        return send(
            bufs[i].at[0, t, kv], bufs[i].at[1, t, kv], zs.at[i, t, kv], zr.at[i, t, kv],
            "seq", zpeer[i],
        )

    def push(i, t, kv):
        total = acc[kv]
        if t >= 1 and (t >= 2 or kv == i):
            ring(i, t - 1, kv).wait_recv()
            total = total + bufs[i][1, t - 1, kv].astype(jnp.float32)
        bufs[i][0, t, kv] = total.astype(jnp.bfloat16)
        ring(i, t, kv).start()

    collect(lax.rem(z + 4, NZ))
    push(0, 0, 0)
    push(1, 0, 1)
    for t in range(1, 4):
        collect(lax.rem(z + 4 - t, NZ))
        push(0, t, 0)
        push(0, t, 1)
        collect(lax.rem(z + 4 + t, NZ))
        push(1, t, 1)
        push(1, t, 0)
    collect(z)
    outs = (dk_ref, dv_ref)
    for kv in range(2):
        total = acc[kv] + wloc[kv]
        for i in range(2):
            ring(i, 3, kv).wait_recv()
            total = total + bufs[i][1, 3, kv].astype(jnp.float32)
        outs[kv][...] = total.astype(jnp.bfloat16)

    for i in range(2):
        for t in range(4):
            for kv in range(2):
                if t == 0 and kv != i:
                    continue
                ring(i, t, kv).wait_send()
    for c in range(NZ):
        for p in range(3):
            slot_copy(p, c).wait_send()
    for p in range(2):
        halo_copy(p).wait_send()

    @pl.when(y != 0)
    def _():
        global_copy(0).wait_send()


QUARTER = D // 4


def project_kernel(
    dq, dk, dv, wq, wk, wv, out, term, pair, xout, xin, ps, pr, xs, xr
):
    h = lax.axis_index("head")
    x = lax.div(h, 2)
    c = lax.rem(h, 2)
    partner = x * 2 + 1 - c
    peers = (lax.rem(x + 1, NX) * 2 + c, lax.rem(x + NX - 1, NX) * 2 + c)
    greet((partner,) + peers, "head")

    def cols(quarter):
        return pl.ds(quarter * QUARTER, QUARTER)

    def pair_copy(d, quarter):
        return send(
            term.at[d, rows_of((1 - c) * BLOCK, BLOCK), cols(quarter)],
            pair.at[d, :, cols(quarter)], ps.at[d, quarter], pr.at[d, quarter],
            "head", partner,
        )

    def ring(i, t, quarter):
        return send(
            xout.at[i, t, :, cols(quarter)], xin.at[i, t, :, cols(quarter)],
            xs.at[i, t, quarter], xr.at[i, t, quarter], "head", peers[i],
        )

    def compute(d):
        at = rows_of(lax.rem(x + d, NX) * 2 * BLOCK, 2 * BLOCK)
        a_q = dq[at, :]
        a_k = dk[at, :]
        a_v = dv[at, :]
        width = 512
        for quarter in range(4):
            def tile(n, carry):
                w = pl.ds(pl.multiple_of(quarter * QUARTER + n * width, width), width)
                total = dot(a_q, wq[w, :], NT) + dot(a_k, wk[w, :], NT) + dot(a_v, wv[w, :], NT)
                term[d, :, w] = total.astype(jnp.bfloat16)
                return carry

            lax.fori_loop(0, QUARTER // width, tile, 0)
            pair_copy(d, quarter).start()

    def both(d, quarter):
        pair_copy(d, quarter).wait_recv()
        mine = term[d, rows_of(c * BLOCK, BLOCK), cols(quarter)].astype(jnp.float32)
        return mine + pair[d, :, cols(quarter)].astype(jnp.float32)

    def arrived(i, t, quarter):
        ring(i, t, quarter).wait_recv()
        return xin[i, t, :, cols(quarter)].astype(jnp.float32)

    def push(i, t, quarter, total):
        xout[i, t, :, cols(quarter)] = total.astype(jnp.bfloat16)
        ring(i, t, quarter).start()

    compute(2)
    compute(1)
    for n in range(2):
        push(0, 0, n, both(2, n))
        push(1, 0, 2 + n, both(2, 2 + n))
    compute(3)
    for n in range(2):
        push(0, 1, 2 + n, both(1, 2 + n))
        push(1, 1, n, both(3, n))
    compute(0)
    for n in range(2):
        push(0, 1, n, both(1, n) + arrived(0, 0, n))
        push(1, 1, 2 + n, both(3, 2 + n) + arrived(1, 0, 2 + n))
    for quarter in (2, 3, 0, 1):
        total = both(0, quarter) + arrived(0, 1, quarter) + arrived(1, 1, quarter)
        out[:, cols(quarter)] = total.astype(jnp.bfloat16)
    for d in range(4):
        for quarter in range(4):
            pair_copy(d, quarter).wait_send()
    for i in range(2):
        for quarter in range(4):
            if quarter // 2 == i:
                ring(i, 0, quarter).wait_send()
            ring(i, 1, quarter).wait_send()


def sds(shape, dtype=jnp.bfloat16):
    return jax.ShapeDtypeStruct(shape, dtype)


DMA = pltpu.SemaphoreType.DMA


def prep(rand_owner, rand_block):
    return pl.pallas_call(
        prep_kernel,
        out_shape=(sds((144,), jnp.int32), sds((64,), jnp.int32), sds((24,), jnp.int32)),
        in_specs=[smem()] * 2,
        out_specs=(smem(),) * 3,
        scratch_shapes=[pltpu.SMEM((128,), jnp.int32)],
        name="prep",
    )(rand_owner, rand_block)


def fetch(picks, keys, values):
    return pl.pallas_call(
        fetch_kernel,
        out_shape=sds((2, TABLE * BLOCK, HD)),
        in_specs=[smem(), vmem(), vmem()],
        out_specs=vmem(),
        scratch_shapes=[
            VM((2, RUN, BLOCK, HD), jnp.bfloat16),
            VM((3, NZ, 2, 2 * BLOCK, HD), jnp.bfloat16),
            DMA((2, 4, 2)),
            DMA((2, 4, 2)),
            DMA((3, NZ)),
            DMA((3, NZ)),
            DMA((2,)),
            DMA((2,)),
            DMA((3,)),
            DMA,
        ],
        compiler_params=pltpu.CompilerParams(collective_id=0, has_side_effects=True),
        name="fetch",
    )(picks, keys, values)


def attend(lists, slots, query, grad_out, table):
    whole = lambda shape: pl.BlockSpec(shape, lambda b, *_: (0,) * len(shape))
    step = pl.BlockSpec((BLOCK, GROUP * HD), lambda b, *_: (b, 0))
    outs = (
        sds((ROWS, GROUP * HD)),
        sds((2, 64 * BLOCK, HD)),
        sds((2, ROWS, HD), jnp.float32),
        sds((2, 2 * BLOCK, HD)),
        sds((2, 2 * BLOCK, HD)),
    )
    return pl.pallas_call(
        attend_kernel,
        out_shape=outs,
        grid_spec=pltpu.PrefetchScalarGridSpec(
            num_scalar_prefetch=2,
            grid=(RUN,),
            in_specs=[step, step, whole((2, TABLE * BLOCK, HD))],
            out_specs=(step,) + tuple(whole(o.shape) for o in outs[1:]),
            scratch_shapes=[
                VM((ROWS, HD), jnp.bfloat16),
                VM((ROWS, HD), jnp.bfloat16),
                VM((2, ROWS + 2 * BLOCK, HD), jnp.float32),
                VM((2, 2 * BLOCK, HD), jnp.float32),
            ],
        ),
        name="attend",
    )(lists, slots, query, grad_out, table)


def give_back(picks, part, wloc, halo, glob):
    return pl.pallas_call(
        return_kernel,
        out_shape=(sds((ROWS, HD)), sds((ROWS, HD))),
        in_specs=[smem()] + [vmem()] * 4,
        out_specs=(vmem(), vmem()),
        scratch_shapes=[
            VM((3, NZ, 2, 2 * BLOCK, HD), jnp.bfloat16),
            VM((2, 2, BLOCK, HD), jnp.bfloat16),
            VM((3, 2, 2 * BLOCK, HD), jnp.bfloat16),
            VM((2, ROWS, HD), jnp.float32),
            VM((2, 4, 2, ROWS, HD), jnp.bfloat16),
            VM((2, 4, 2, ROWS, HD), jnp.bfloat16),
            DMA((2, 4, 2)),
            DMA((2, 4, 2)),
            DMA((3, NZ)),
            DMA((3, NZ)),
            DMA((2,)),
            DMA((2,)),
            DMA,
            DMA((3,)),
        ],
        compiler_params=pltpu.CompilerParams(collective_id=1, has_side_effects=True),
        name="give_back",
    )(picks, part, wloc, halo, glob)


def project(dq, dk, dv, wq, wk, wv):
    return pl.pallas_call(
        project_kernel,
        out_shape=sds((BLOCK, D)),
        in_specs=[vmem()] * 6,
        out_specs=vmem(),
        scratch_shapes=[
            VM((4, 2 * BLOCK, D), jnp.bfloat16),
            VM((4, BLOCK, D), jnp.bfloat16),
            VM((2, 2, BLOCK, D), jnp.bfloat16),
            VM((2, 2, BLOCK, D), jnp.bfloat16),
            DMA((4, 4)),
            DMA((4, 4)),
            DMA((2, 2, 4)),
            DMA((2, 2, 4)),
        ],
        compiler_params=pltpu.CompilerParams(collective_id=2, has_side_effects=True),
        name="project",
    )(dq, dk, dv, wq, wk, wv)


def on_device(query, keys, values, grad_out, w_query, w_key, w_value, rand_owner, rand_block):
    picks, lists, slots = prep(rand_owner, rand_block)
    table = fetch(picks, keys, values)
    dq, part, wloc, halo, glob = attend(lists, slots, query, grad_out, table)
    dk, dv = give_back(picks, part, wloc, halo, glob)
    return project(dq, dk, dv, w_query, w_key, w_value)


def solution(mesh):
    return jax.shard_map(
        on_device,
        mesh=mesh,
        in_specs=(
            P("seq", "head"),
            P("seq", "head"),
            P("seq", "head"),
            P("seq", "head"),
            P(None, "head"),
            P(None, "head"),
            P(None, "head"),
            P(),
            P(),
        ),
        out_specs=P(("seq", "head"), None),
        check_vma=False,
    )
```

```python
import functools

import jax
import jax.numpy as jnp
from jax import lax
from jax.experimental import pallas as pl
from jax.experimental.pallas import tpu as pltpu
from jax.sharding import PartitionSpec as P

BLOCK = 64
HD = 128
NZ = 8
NY = 4
NX = 4
RUN = 8
ROWS = RUN * BLOCK
GROUP = 4
D = 4096
FROM_UP = NZ * RUN
FROM_DOWN = FROM_UP + 3 * NZ
FROM_FAR = FROM_DOWN + 3 * NZ
EXTRA = FROM_FAR + 2 * NZ
TABLE = EXTRA + 4
OUT_UP = 2 * NZ
OUT_DOWN = OUT_UP + 3 * NZ
OUT = OUT_DOWN + 3 * NZ
MESH = pl.DeviceIdType.MESH
SCALE = HD ** (-0.5)
VM = pltpu.VMEM
DMA = pltpu.SemaphoreType.DMA
NT = (((1,), (1,)), ((), ()))
NN = (((1,), (0,)), ((), ()))
TN = (((0,), (0,)), ((), ()))


def vmem():
    return pl.BlockSpec(memory_space=pltpu.VMEM)


def smem():
    return pl.BlockSpec(memory_space=pltpu.SMEM)


def sds(shape, dtype=jnp.bfloat16):
    return jax.ShapeDtypeStruct(shape, dtype)


def dot(a, b, dims):
    return lax.dot_general(a, b, dims, preferred_element_type=jnp.float32)


def seq_place():
    s = lax.axis_index("seq")
    return s, lax.div(s, NY), lax.rem(s, NY)


def rows_of(start, size):
    return pl.ds(pl.multiple_of(start, BLOCK), size)


def neighbours(z, y):
    return (
        lax.rem(z + 1, NZ) * NY + y,
        lax.rem(z + NZ - 1, NZ) * NY + y,
        z * NY + lax.rem(y + 1, NY),
        z * NY + lax.rem(y + 3, NY),
        z * NY + lax.rem(y + 2, NY),
    )


def greet(peers):
    barrier = pltpu.get_barrier_semaphore()
    for axis, peer in peers:
        pl.semaphore_signal(barrier, inc=1, device_id={axis: peer}, device_id_type=MESH)
    pl.semaphore_wait(barrier, len(peers))


def send(src, dst, ssem, rsem, axis, peer):
    return pltpu.make_async_remote_copy(
        src_ref=src,
        dst_ref=dst,
        send_sem=ssem,
        recv_sem=rsem,
        device_id={axis: peer},
        device_id_type=MESH,
    )


def group_prefix(value, lane):
    for shift in (1, 2, 4):
        value = value + jnp.where(lane >= shift, pltpu.roll(value, shift, 1), 0)
    return value


def index_tables(owner_ref, block_ref, z, y):
    low = z < NZ // 2
    owners = jnp.where(low, owner_ref[:, :128], owner_ref[:, 128:])
    picks = jnp.where(low, block_ref[:, :128], block_ref[:, 128:])
    shape = (NZ * NY, 128)
    index = lax.broadcasted_iota(jnp.int32, shape, 0)
    lane = lax.broadcasted_iota(jnp.int32, shape, 1) & 7
    hits = [jnp.broadcast_to(owners[j : j + 1], shape) == index for j in range(3)]
    named = jnp.zeros(shape, jnp.int32)
    chosen = jnp.zeros(shape, jnp.int32)
    for j in range(3):
        named = named + jnp.where(hits[j], 1, 0)
        chosen = chosen + jnp.where(hits[j], jnp.broadcast_to(picks[j : j + 1], shape), 0)
    place = group_prefix(named, lane) - named
    tables = []
    for k in range(2):
        mine = jnp.where((named == 1) & (place == k), chosen + 1, 0)
        tables.append(group_prefix(mine, lane) - 1)
    rows = []
    slots = []
    for j in range(3):
        owner = owners[j : j + 1]
        at = jnp.sum(jnp.where(hits[j], place, 0), axis=0, keepdims=True)
        zo = owner >> 2
        rel = ((owner & 3) - y + NY) & 3
        rows.append(
            jnp.where(
                rel == 0,
                zo * RUN + picks[j : j + 1],
                jnp.where(
                    rel == 2,
                    FROM_FAR + zo * 2 + at,
                    jnp.where(rel == 1, FROM_UP, FROM_DOWN) + zo * 3 + at,
                ),
            )
        )
        slots.append(
            jnp.where(
                rel == 0,
                zo * 2 + at,
                jnp.where(
                    rel == 2,
                    jnp.where(at == 0, OUT_UP, OUT_DOWN) + zo * 3 + 2,
                    jnp.where(rel == 1, OUT_UP, OUT_DOWN) + zo * 3 + at,
                ),
            )
        )
    return tables, rows, slots


def fetch_kernel(
    owner_ref, block_ref, k_ref, v_ref, tab, picks_ref, lists_ref,
    safe_vmem, safe, stage, sendbuf, ts, zs, zr, ys, yr, fs, fr, hs, hr, gs, gr
):
    s, z, y = seq_place()
    zu, zd, yp, ym, y2 = neighbours(z, y)
    ypeers = (yp, ym, y2)
    own = (k_ref, v_ref)
    greet([("seq", n) for n in (zu, zd, yp, ym, y2)])

    def ring(up, t, kv):
        chunk = lax.rem(z + (NZ - t if up else t), NZ)
        where = tab.at[kv, rows_of(chunk * ROWS, ROWS)]
        i = 0 if up else 1
        return send(
            own[kv] if t == 0 else where, where, zs.at[i, t, kv], zr.at[i, t, kv],
            "seq", zu if up else zd,
        )

    def landed(up, t, kv):
        chunk = lax.rem(z + (NZ - 1 - t if up else 1 + t), NZ)
        where = tab.at[kv, rows_of(chunk * ROWS, ROWS)]
        i = 0 if up else 1
        return send(where, where, zs.at[i, t, kv], zr.at[i, t, kv], "seq", zu if up else zd)

    def slot_copy(p, chunk):
        first = (FROM_DOWN, FROM_UP)[p]
        at = rows_of((first + chunk * 3) * BLOCK, 3 * BLOCK)
        return send(
            sendbuf.at[p, chunk], tab.at[:, at, :], ys.at[p, chunk], yr.at[p, chunk],
            "seq", ypeers[p],
        )

    def relay(p, chunk):
        first = (FROM_DOWN, FROM_UP)[p]
        src = rows_of((first + chunk * 3 + 2) * BLOCK, BLOCK)
        at = rows_of((FROM_FAR + chunk * 2 + p) * BLOCK, BLOCK)
        return send(
            tab.at[:, src, :], tab.at[:, at, :], fs.at[p, chunk], fr.at[p, chunk],
            "seq", ypeers[p],
        )

    def global_copy(p):
        return send(
            tab.at[:, pl.ds(0, 2 * BLOCK), :],
            tab.at[:, pl.ds((EXTRA + 2) * BLOCK, 2 * BLOCK), :],
            gs.at[p], gr, "seq", ypeers[p],
        )

    def halo_copy(p):
        if p == 0:
            row = lax.rem(z + NZ - lax.div(y, 3), NZ) * ROWS + (RUN - 1) * BLOCK
        else:
            row = lax.rem(z + lax.div(3 - y, 3), NZ) * ROWS
        at = pl.ds((EXTRA + p) * BLOCK, BLOCK)
        return send(
            tab.at[:, rows_of(row, BLOCK), :], tab.at[:, at, :], hs.at[p], hr.at[p],
            "seq", ypeers[p],
        )

    plane = lax.rem(z, NZ // 2) * (NY * RUN) + RUN - 1

    def spread(chunk):
        for kv in range(2):
            stage[kv] = tab[kv, rows_of(chunk * ROWS, ROWS), :].reshape(RUN, BLOCK, HD)
        for p in range(2):
            wants = [(1 if p == 0 else 3, 0), (1 if p == 0 else 3, 1), (2, p)]
            for n, (rel, k) in enumerate(wants):
                lane = plane + lax.rem(y + rel, NY) * RUN
                pick = safe[k * NZ * NY + chunk * NY + y, lane]
                for kv in range(2):
                    sendbuf[p, chunk, kv, n * BLOCK : (n + 1) * BLOCK, :] = stage[kv, pick]
        for p in range(2):
            slot_copy(p, chunk).start()

        @pl.when(jnp.logical_and(chunk == 0, y == 0))
        def _():
            for p in range(3):
                global_copy(p).start()

    def pass_on(chunk):
        for p in range(2):
            slot_copy(p, chunk).wait_recv()
        for p in range(2):
            relay(p, chunk).start()

    for kv in range(2):
        ring(True, 0, kv).start()
        ring(False, 0, kv).start()
    tables, rows, slots = index_tables(owner_ref, block_ref, z, y)
    for k in range(2):
        part = slice(k * NZ * NY, (k + 1) * NZ * NY)
        picks_ref[part, :] = tables[k]
        safe_vmem[part, :] = jnp.maximum(tables[k], 0)
    to_scalar = pltpu.make_async_copy(safe_vmem, safe, ts)
    to_scalar.start()
    for j in range(3):
        lists_ref[j : j + 1, :] = rows[j]
        lists_ref[3 + j : 4 + j, :] = slots[j]
    for kv in range(2):
        tab[kv, rows_of(z * ROWS, ROWS), :] = own[kv][...]
    to_scalar.wait()
    spread(z)
    before = [z]
    for t in range(4):
        for kv in range(2):
            for up in (True, False):
                if t == 3 and kv != (0 if up else 1):
                    continue
                landed(up, t, kv).wait_recv()
                if t < 2 or (t == 2 and kv == (0 if up else 1)):
                    ring(up, t + 1, kv).start()
        for chunk in before:
            pass_on(chunk)
        if t == 0:
            halo_copy(0).start()
            halo_copy(1).start()
        before = [lax.rem(z + NZ - 1 - t, NZ)]
        if t < 3:
            before.append(lax.rem(z + 1 + t, NZ))
        for chunk in before:
            spread(chunk)
    for chunk in before:
        pass_on(chunk)

    for p in range(2):
        for c in range(NZ):
            relay(p, c).wait_recv()
        halo_copy(p).wait_recv()

    @pl.when(y == 0)
    def _():
        for kv in range(2):
            tab[kv, (EXTRA + 2) * BLOCK : (EXTRA + 4) * BLOCK, :] = tab[kv, 0 : 2 * BLOCK, :]
        for p in range(3):
            global_copy(p).wait_send()

    @pl.when(y != 0)
    def _():
        global_copy(0).wait_recv()

    for t in range(4):
        for kv in range(2):
            for up in (True, False):
                if t == 3 and kv != (0 if up else 1):
                    continue
                ring(up, t, kv).wait_send()
    for p in range(2):
        for c in range(NZ):
            slot_copy(p, c).wait_send()
            relay(p, c).wait_send()
        halo_copy(p).wait_send()


PER = 2


def attend_kernel(
    lists, q_ref, do_ref, tab, dq_ref, part, wloc, halo, glob, kl, vl, wacc, gacc
):
    step = pl.program_id(0)
    s, z, y = seq_place()
    lane0 = (lax.rem(z, NZ // 2) * NY + y) * RUN

    @pl.when(step == 0)
    def _():
        wacc[...] = jnp.zeros_like(wacc)
        gacc[...] = jnp.zeros_like(gacc)

    grads = []
    for n in range(PER):
        b = step * PER + n
        index = [
            jnp.where(b == 0, EXTRA, z * RUN + b - 1),
            z * RUN + b,
            jnp.where(b == RUN - 1, EXTRA + 1, z * RUN + b + 1),
            EXTRA + 2,
            EXTRA + 3,
        ] + [lists[j, lane0 + b] for j in range(3)]
        for j in range(8):
            at = rows_of(index[j] * BLOCK, BLOCK)
            kl[n, j * BLOCK : (j + 1) * BLOCK, :] = tab[0, at, :]
            vl[n, j * BLOCK : (j + 1) * BLOCK, :] = tab[1, at, :]
    for n in range(PER):
        b = step * PER + n
        mine = slice(n * BLOCK, (n + 1) * BLOCK)
        q4 = jnp.concatenate([q_ref[mine, g * HD : (g + 1) * HD] for g in range(GROUP)], axis=0)
        d4 = jnp.concatenate([do_ref[mine, g * HD : (g + 1) * HD] for g in range(GROUP)], axis=0)
        keys = kl[n]
        vals = vl[n]
        scores = dot(keys, q4, NT)
        no_left = jnp.logical_and(s == 0, b == 0)
        no_right = jnp.logical_and(s == NZ * NY - 1, b == RUN - 1)
        scores = jnp.concatenate(
            [
                jnp.where(no_left, -1e30, scores[:BLOCK]),
                scores[BLOCK : 2 * BLOCK],
                jnp.where(no_right, -1e30, scores[2 * BLOCK : 3 * BLOCK]),
                scores[3 * BLOCK :],
            ],
            axis=0,
        )
        row_max = jnp.max(scores, axis=0, keepdims=True)
        powers = jnp.exp((scores - row_max) * SCALE)
        weights = powers * (1.0 / jnp.sum(powers, axis=0, keepdims=True))
        weights_half = weights.astype(jnp.bfloat16)
        dprob = dot(vals, d4, NT)
        delta = jnp.sum(weights_half.astype(jnp.float32) * dprob, axis=0, keepdims=True)
        dscore_half = (weights * (dprob - delta)).astype(jnp.bfloat16)
        dq = (dot(dscore_half, keys, TN) * SCALE).astype(jnp.bfloat16)
        for g in range(GROUP):
            dq_ref[mine, g * HD : (g + 1) * HD] = dq[g * BLOCK : (g + 1) * BLOCK]
        grads.append((dot(dscore_half, q4, NN) * SCALE, dot(weights_half, d4, NN)))
    for n in range(PER):
        b = step * PER + n
        for kv in range(2):
            grad = grads[n][kv]
            wacc[kv, rows_of(b * BLOCK, 3 * BLOCK), :] += grad[: 3 * BLOCK]
            gacc[kv] += grad[3 * BLOCK : 5 * BLOCK]
            for j in range(3):
                at = rows_of(lists[3 + j, lane0 + b] * BLOCK, BLOCK)
                part[kv, at, :] = grad[(5 + j) * BLOCK : (6 + j) * BLOCK].astype(jnp.bfloat16)

    @pl.when(step == RUN // PER - 1)
    def _():
        for kv in range(2):
            wloc[kv] = wacc[kv, BLOCK : BLOCK + ROWS, :]
            halo[kv, :BLOCK, :] = wacc[kv, :BLOCK, :].astype(jnp.bfloat16)
            halo[kv, BLOCK:, :] = wacc[kv, BLOCK + ROWS :, :].astype(jnp.bfloat16)
            glob[kv] = gacc[kv].astype(jnp.bfloat16)


QUARTER = D // 4
TILE = 512


def finish_kernel(
    picks_ref, part, wloc, halo, glob, dq, wq_hbm, wk_hbm, wv_hbm, out,
    wq, wkv, dkv, ybuf, fbuf, hbuf, gbuf, acc, zup, zdown,
    total_ref, term, pair, xout, xin,
    ws, zs, zr, ys, yr, fs, fr, hs, hr, gs, gr, ps, pr, xs, xr
):
    s, z, y = seq_place()
    zu, zd, yp, ym, y2 = neighbours(z, y)
    ypeers = (yp, ym)
    h = lax.axis_index("head")
    x = lax.div(h, 2)
    c = lax.rem(h, 2)
    partner = x * 2 + 1 - c
    xpeers = (lax.rem(x + 1, NX) * 2 + c, lax.rem(x + NX - 1, NX) * 2 + c)
    loads = (
        pltpu.make_async_copy(wq_hbm, wq, ws.at[0]),
        pltpu.make_async_copy(wk_hbm, wkv.at[:, pl.ds(0, HD)], ws.at[1]),
        pltpu.make_async_copy(wv_hbm, wkv.at[:, pl.ds(HD, HD)], ws.at[2]),
    )
    for load in loads:
        load.start()
    greet(
        [("seq", n) for n in (zu, zd, yp, ym, y2)]
        + [("head", n) for n in (partner,) + xpeers]
    )

    def slot_copy(p, chunk):
        first = (OUT_UP, OUT_DOWN)[p]
        at = rows_of((first + chunk * 3) * BLOCK, 3 * BLOCK)
        return send(
            part.at[:, at, :], ybuf.at[p, chunk], ys.at[p, chunk], yr.at[p, chunk],
            "seq", ypeers[p],
        )

    def relay(p, chunk):
        return send(
            ybuf.at[p, chunk, :, pl.ds(2 * BLOCK, BLOCK), :], fbuf.at[p, chunk],
            fs.at[p, chunk], fr.at[p, chunk], "seq", ypeers[p],
        )

    def halo_copy(p):
        half = pl.ds(BLOCK if p == 0 else 0, BLOCK)
        return send(halo.at[:, half, :], hbuf.at[p], hs.at[p], hr.at[p], "seq", ypeers[p])

    def global_copy(slot):
        return send(glob, gbuf.at[slot], gs, gr.at[slot], "seq", z * NY)

    chunks = [lax.rem(z + off + NZ, NZ) for off in (4, 3, -3, 2, -2, 1, -1, 0)]
    low_chunk = lax.rem(z + NZ - lax.div(y, 3), NZ)
    high_chunk = lax.rem(z + lax.div(3 - y, 3), NZ)
    plane = lax.rem(z, NZ // 2) * (NY * RUN) + RUN - 1

    def offer(n):
        for p in range(2):
            slot_copy(p, chunks[n]).start()

    def pass_on(n):
        for p in range(2):
            slot_copy(p, chunks[n]).wait_recv()
        for p in range(2):
            relay(p, chunks[n]).start()

    def collect(n):
        chunk = chunks[n]
        for p in range(2):
            relay(p, chunk).wait_recv()
        pieces = []
        for k in range(2):
            pieces.append((0, k, lambda kv, k=k: part[kv, rows_of((chunk * 2 + k) * BLOCK, BLOCK), :]))
            pieces.append((3, k, lambda kv, k=k: ybuf[0, chunk, kv, k * BLOCK : (k + 1) * BLOCK, :]))
            pieces.append((1, k, lambda kv, k=k: ybuf[1, chunk, kv, k * BLOCK : (k + 1) * BLOCK, :]))
            pieces.append((2, k, lambda kv, k=k: fbuf[k, chunk, kv]))
        picks = [
            picks_ref[k * NZ * NY + chunk * NY + y, plane + lax.rem(y + rel, NY) * RUN]
            for rel, k, _ in pieces
        ]
        for kv in range(2):
            data = [get(kv).astype(jnp.float32) for _, _, get in pieces]

            def one(b, carry):
                total = jnp.where(picks[0] == b, data[0], 0.0)
                for i in range(1, 8):
                    total = total + jnp.where(picks[i] == b, data[i], 0.0)
                acc[kv, rows_of(b * BLOCK, BLOCK), :] = total
                return carry

            lax.fori_loop(0, RUN, one, 0)
        last = pl.ds((RUN - 1) * BLOCK, BLOCK)
        first = pl.ds(0, BLOCK)

        @pl.when(chunk == low_chunk)
        def _():
            for kv in range(2):
                acc[kv, last, :] += hbuf[1, kv].astype(jnp.float32)

        @pl.when(chunk == high_chunk)
        def _():
            for kv in range(2):
                acc[kv, first, :] += hbuf[0, kv].astype(jnp.float32)

        @pl.when(jnp.logical_and(chunk == 0, y == 0))
        def _():
            for kv in range(2):
                total = glob[kv].astype(jnp.float32)
                for m in range(3):
                    total = total + gbuf[m, kv].astype(jnp.float32)
                acc[kv, 0 : 2 * BLOCK, :] += total

    bufs = (zup, zdown)
    zpeer = (zu, zd)

    def zring(i, t, kv):
        return send(
            bufs[i].at[0, t, kv], bufs[i].at[1, t, kv], zs.at[i, t, kv], zr.at[i, t, kv],
            "seq", zpeer[i],
        )

    def zpush(i, t, kv):
        total = acc[kv]
        if t >= 1 and (t >= 2 or kv == i):
            zring(i, t - 1, kv).wait_recv()
            total = total + bufs[i][1, t - 1, kv].astype(jnp.float32)
        bufs[i][0, t, kv] = total.astype(jnp.bfloat16)
        zring(i, t, kv).start()

    def token_rows(d):
        return rows_of(lax.rem(x + d, NX) * 2 * BLOCK, 2 * BLOCK)

    def query_part(d):
        a = dq[token_rows(d), :]

        def tile(n, carry):
            w = pl.ds(pl.multiple_of(n * TILE, TILE), TILE)
            total_ref[d, :, w] = dot(a, wq[w, :], NT)
            return carry

        lax.fori_loop(0, D // TILE, tile, 0)

    halo_copy(0).start()
    halo_copy(1).start()
    offer(0)
    for n in range(1, NY):
        @pl.when(y == n)
        def _():
            global_copy(n - 1).start()
    offer(1)
    for load in loads:
        load.wait()
    query_part(2)
    pass_on(0)
    offer(2)
    for p in range(2):
        halo_copy(p).wait_recv()

    @pl.when(y == 0)
    def _():
        for m in range(3):
            global_copy(m).wait_recv()

    pass_on(1)
    offer(3)
    collect(0)
    zpush(0, 0, 0)
    zpush(1, 0, 1)
    pass_on(2)
    offer(4)
    for t in range(1, 4):
        n = 2 * t - 1
        collect(n)
        zpush(0, t, 0)
        zpush(0, t, 1)
        pass_on(n + 2) if n + 2 < NZ else None
        offer(n + 4) if n + 4 < NZ else None
        collect(n + 1)
        zpush(1, t, 1)
        zpush(1, t, 0)
        pass_on(n + 3) if n + 3 < NZ else None
        offer(n + 5) if n + 5 < NZ else None
        query_part((1, 3, 0)[t - 1])
    collect(7)
    for kv in range(2):
        total = acc[kv] + wloc[kv]
        for i in range(2):
            zring(i, 3, kv).wait_recv()
            total = total + bufs[i][1, 3, kv].astype(jnp.float32)
        dkv[:, kv * HD : (kv + 1) * HD] = total.astype(jnp.bfloat16)

    def cols(quarter):
        return pl.ds(quarter * QUARTER, QUARTER)

    def pair_copy(d, quarter):
        return send(
            term.at[d, rows_of((1 - c) * BLOCK, BLOCK), cols(quarter)],
            pair.at[d, :, cols(quarter)], ps.at[d, quarter], pr.at[d, quarter],
            "head", partner,
        )

    def xring(i, t, quarter):
        return send(
            xout.at[i, t, :, cols(quarter)], xin.at[i, t, :, cols(quarter)],
            xs.at[i, t, quarter], xr.at[i, t, quarter], "head", xpeers[i],
        )

    def compute(d):
        a = dkv[token_rows(d), :]
        for quarter in range(4):
            def tile(n, carry):
                w = pl.ds(pl.multiple_of(quarter * QUARTER + n * TILE, TILE), TILE)
                total = total_ref[d, :, w] + dot(a, wkv[w, :], NT)
                term[d, :, w] = total.astype(jnp.bfloat16)
                return carry

            lax.fori_loop(0, QUARTER // TILE, tile, 0)
            pair_copy(d, quarter).start()

    def both(d, quarter):
        pair_copy(d, quarter).wait_recv()
        mine = term[d, rows_of(c * BLOCK, BLOCK), cols(quarter)].astype(jnp.float32)
        return mine + pair[d, :, cols(quarter)].astype(jnp.float32)

    def arrived(i, t, quarter):
        xring(i, t, quarter).wait_recv()
        return xin[i, t, :, cols(quarter)].astype(jnp.float32)

    def xpush(i, t, quarter, total):
        xout[i, t, :, cols(quarter)] = total.astype(jnp.bfloat16)
        xring(i, t, quarter).start()

    compute(2)
    compute(1)
    for n in range(2):
        xpush(0, 0, n, both(2, n))
        xpush(1, 0, 2 + n, both(2, 2 + n))
    compute(3)
    for n in range(2):
        xpush(0, 1, 2 + n, both(1, 2 + n))
        xpush(1, 1, n, both(3, n))
    compute(0)
    for n in range(2):
        xpush(0, 1, n, both(1, n) + arrived(0, 0, n))
        xpush(1, 1, 2 + n, both(3, 2 + n) + arrived(1, 0, 2 + n))
    for quarter in (2, 3, 0, 1):
        total = both(0, quarter) + arrived(0, 1, quarter) + arrived(1, 1, quarter)
        out[:, cols(quarter)] = total.astype(jnp.bfloat16)

    for i in range(2):
        for t in range(4):
            for kv in range(2):
                if t == 0 and kv != i:
                    continue
                zring(i, t, kv).wait_send()
    for p in range(2):
        for n in range(NZ):
            slot_copy(p, n).wait_send()
            relay(p, n).wait_send()
        halo_copy(p).wait_send()

    @pl.when(y != 0)
    def _():
        global_copy(0).wait_send()

    for d in range(4):
        for quarter in range(4):
            pair_copy(d, quarter).wait_send()
    for i in range(2):
        for quarter in range(4):
            if quarter // 2 == i:
                xring(i, 0, quarter).wait_send()
            xring(i, 1, quarter).wait_send()


def fetch(owners, blocks, keys, values):
    return pl.pallas_call(
        fetch_kernel,
        out_shape=(
            sds((2, TABLE * BLOCK, HD)),
            sds((2 * NZ * NY, 128), jnp.int32),
            sds((8, 128), jnp.int32),
        ),
        in_specs=[vmem()] * 4,
        out_specs=(vmem(),) * 3,
        scratch_shapes=[
            VM((2 * NZ * NY, 128), jnp.int32),
            pltpu.SMEM((2 * NZ * NY, 128), jnp.int32),
            VM((2, RUN, BLOCK, HD), jnp.bfloat16),
            VM((2, NZ, 2, 3 * BLOCK, HD), jnp.bfloat16),
            DMA,
            DMA((2, 4, 2)),
            DMA((2, 4, 2)),
            DMA((2, NZ)),
            DMA((2, NZ)),
            DMA((2, NZ)),
            DMA((2, NZ)),
            DMA((2,)),
            DMA((2,)),
            DMA((3,)),
            DMA,
        ],
        compiler_params=pltpu.CompilerParams(collective_id=0, has_side_effects=True),
        name="fetch",
    )(owners, blocks, keys, values)


def attend(lists, query, grad_out, table):
    whole = lambda shape: pl.BlockSpec(shape, lambda b, *_: (0,) * len(shape))
    step = pl.BlockSpec((PER * BLOCK, GROUP * HD), lambda b, *_: (b, 0))
    outs = (
        sds((ROWS, GROUP * HD)),
        sds((2, OUT * BLOCK, HD)),
        sds((2, ROWS, HD), jnp.float32),
        sds((2, 2 * BLOCK, HD)),
        sds((2, 2 * BLOCK, HD)),
    )
    return pl.pallas_call(
        attend_kernel,
        out_shape=outs,
        grid_spec=pltpu.PrefetchScalarGridSpec(
            num_scalar_prefetch=1,
            grid=(RUN // PER,),
            in_specs=[step, step, whole((2, TABLE * BLOCK, HD))],
            out_specs=(step,) + tuple(whole(o.shape) for o in outs[1:]),
            scratch_shapes=[
                VM((PER, ROWS, HD), jnp.bfloat16),
                VM((PER, ROWS, HD), jnp.bfloat16),
                VM((2, ROWS + 2 * BLOCK, HD), jnp.float32),
                VM((2, 2 * BLOCK, HD), jnp.float32),
            ],
        ),
        name="attend",
    )(lists, query, grad_out, table)


def finish(picks, part, wloc, halo, glob, dq, wq, wk, wv):
    anywhere = pl.BlockSpec(memory_space=pl.ANY)
    return pl.pallas_call(
        finish_kernel,
        out_shape=sds((BLOCK, D)),
        in_specs=[smem()] + [vmem()] * 5 + [anywhere] * 3,
        out_specs=vmem(),
        scratch_shapes=[
            VM((D, GROUP * HD), jnp.bfloat16),
            VM((D, 2 * HD), jnp.bfloat16),
            VM((ROWS, 2 * HD), jnp.bfloat16),
            VM((2, NZ, 2, 3 * BLOCK, HD), jnp.bfloat16),
            VM((2, NZ, 2, BLOCK, HD), jnp.bfloat16),
            VM((2, 2, BLOCK, HD), jnp.bfloat16),
            VM((3, 2, 2 * BLOCK, HD), jnp.bfloat16),
            VM((2, ROWS, HD), jnp.float32),
            VM((2, 4, 2, ROWS, HD), jnp.bfloat16),
            VM((2, 4, 2, ROWS, HD), jnp.bfloat16),
            VM((4, 2 * BLOCK, D), jnp.float32),
            VM((4, 2 * BLOCK, D), jnp.bfloat16),
            VM((4, BLOCK, D), jnp.bfloat16),
            VM((2, 2, BLOCK, D), jnp.bfloat16),
            VM((2, 2, BLOCK, D), jnp.bfloat16),
            DMA((3,)),
            DMA((2, 4, 2)),
            DMA((2, 4, 2)),
            DMA((2, NZ)),
            DMA((2, NZ)),
            DMA((2, NZ)),
            DMA((2, NZ)),
            DMA((2,)),
            DMA((2,)),
            DMA,
            DMA((3,)),
            DMA((4, 4)),
            DMA((4, 4)),
            DMA((2, 2, 4)),
            DMA((2, 2, 4)),
        ],
        compiler_params=pltpu.CompilerParams(collective_id=1, has_side_effects=True),
        name="finish",
    )(picks, part, wloc, halo, glob, dq, wq, wk, wv)


def on_device(query, keys, values, grad_out, w_query, w_key, w_value, rand_owner, rand_block):
    table, picks, lists = fetch(rand_owner.T, rand_block.T, keys, values)
    dq, part, wloc, halo, glob = attend(lists, query, grad_out, table)
    return finish(picks, part, wloc, halo, glob, dq, w_query, w_key, w_value)


def solution(mesh):
    return jax.shard_map(
        on_device,
        mesh=mesh,
        in_specs=(
            P("seq", "head"),
            P("seq", "head"),
            P("seq", "head"),
            P("seq", "head"),
            P(None, "head"),
            P(None, "head"),
            P(None, "head"),
            P(),
            P(),
        ),
        out_specs=P(("seq", "head"), None),
        check_vma=False,
    )
```

```python
import functools

import jax
import jax.numpy as jnp
from jax import lax
from jax.experimental import pallas as pl
from jax.experimental.pallas import tpu as pltpu
from jax.sharding import PartitionSpec as P

BLOCK = 64
HD = 128
NZ = 8
NY = 4
NX = 4
RUN = 8
ROWS = RUN * BLOCK
GROUP = 4
D = 4096
FROM_UP = NZ * RUN
FROM_DOWN = FROM_UP + 2 * NZ
FROM_FAR = FROM_DOWN + 2 * NZ
EXTRA = FROM_FAR + 2 * NZ
TABLE = EXTRA + 4
OWNERS = NZ * NY
RAW = 2 * OWNERS
ENTRY = 4 * OWNERS
LISTS = 6 * OWNERS
QUARTER = D // 4
TILE = 512
PER = 2
MESH = pl.DeviceIdType.MESH
SCALE = HD ** (-0.5)
VM = pltpu.VMEM
DMA = pltpu.SemaphoreType.DMA
NT = (((1,), (1,)), ((), ()))
NN = (((1,), (0,)), ((), ()))
TN = (((0,), (0,)), ((), ()))


def vmem():
    return pl.BlockSpec(memory_space=pltpu.VMEM)


def sds(shape, dtype=jnp.bfloat16):
    return jax.ShapeDtypeStruct(shape, dtype)


def dot(a, b, dims):
    return lax.dot_general(a, b, dims, preferred_element_type=jnp.float32)


def seq_place():
    s = lax.axis_index("seq")
    return s, lax.div(s, NY), lax.rem(s, NY)


def rows_of(start, size):
    return pl.ds(pl.multiple_of(start, BLOCK), size)


def neighbours(z, y):
    return (
        lax.rem(z + 1, NZ) * NY + y,
        lax.rem(z + NZ - 1, NZ) * NY + y,
        z * NY + lax.rem(y + 1, NY),
        z * NY + lax.rem(y + 3, NY),
        z * NY + lax.rem(y + 2, NY),
    )


def greet(peers):
    barrier = pltpu.get_barrier_semaphore()
    for axis, peer in peers:
        pl.semaphore_signal(barrier, inc=1, device_id={axis: peer}, device_id_type=MESH)
    pl.semaphore_wait(barrier, len(peers))


def send(src, dst, ssem, rsem, axis, peer):
    return pltpu.make_async_remote_copy(
        src_ref=src,
        dst_ref=dst,
        send_sem=ssem,
        recv_sem=rsem,
        device_id={axis: peer},
        device_id_type=MESH,
    )


def group_prefix(value, lane):
    for shift in (1, 2, 4):
        value = value + jnp.where(lane >= shift, pltpu.roll(value, shift, 1), 0)
    return value


def index_tables(owner_ref, block_ref, out, z, y):
    low = z < NZ // 2
    owners = jnp.where(low, owner_ref[:, :128], owner_ref[:, 128:])
    picks = jnp.where(low, block_ref[:, :128], block_ref[:, 128:])
    shape = (OWNERS, 128)
    index = lax.broadcasted_iota(jnp.int32, shape, 0)
    lane = lax.broadcasted_iota(jnp.int32, shape, 1) & 7
    hits = [jnp.broadcast_to(owners[j : j + 1], shape) == index for j in range(3)]
    named = jnp.zeros(shape, jnp.int32)
    chosen = jnp.zeros(shape, jnp.int32)
    entry = lane * 3
    for j in range(3):
        named = named + jnp.where(hits[j], 1, 0)
        chosen = chosen + jnp.where(hits[j], jnp.broadcast_to(picks[j : j + 1], shape), 0)
        entry = entry + jnp.where(hits[j], j, 0)
    place = group_prefix(named, lane) - named
    for k in range(2):
        mine = (named == 1) & (place == k)
        pick = group_prefix(jnp.where(mine, chosen + 1, 0), lane) - 1
        out[k * OWNERS : (k + 1) * OWNERS, :] = jnp.maximum(pick, 0)
        out[RAW + k * OWNERS : RAW + (k + 1) * OWNERS, :] = pick
        out[ENTRY + k * OWNERS : ENTRY + (k + 1) * OWNERS, :] = group_prefix(
            jnp.where(mine, entry, 0), lane
        )
    for j in range(3):
        owner = owners[j : j + 1]
        at = jnp.minimum(jnp.sum(jnp.where(hits[j], place, 0), axis=0, keepdims=True), 1)
        zo = owner >> 2
        rel = ((owner & 3) - y + NY) & 3
        first = jnp.where(rel == 1, FROM_UP, jnp.where(rel == 2, FROM_FAR, FROM_DOWN))
        out[LISTS + j : LISTS + j + 1, :] = jnp.where(
            rel == 0, zo * RUN + picks[j : j + 1], first + zo * 2 + at
        )


def whole_kernel(
    owner_ref, block_ref, k_ref, v_ref, q_hbm, do_hbm, wq_hbm, wk_hbm, wv_hbm, out,
    tables, idx, tab, stage, ysend, q_ref, do_ref, dq_ref, kl, vl, wacc, gacc, rp,
    halo, glob, wq, wkv, dkv, rsend, ybuf, hbuf, gbuf, acc, zup, zdown,
    total_ref, term, pair, xout, xin,
    ts, ws, zs, zr, ys, yr, hs, hr, gs, gr,
    zs2, zr2, ys2, yr2, hs2, hr2, gs2, gr2, ps, pr, xs, xr
):
    s, z, y = seq_place()
    zu, zd, yp, ym, y2 = neighbours(z, y)
    ypeers = (yp, ym, y2)
    h = lax.axis_index("head")
    x = lax.div(h, 2)
    c = lax.rem(h, 2)
    partner = x * 2 + 1 - c
    xpeers = (lax.rem(x + 1, NX) * 2 + c, lax.rem(x + NX - 1, NX) * 2 + c)
    plane = lax.rem(z, NZ // 2) * (NY * RUN) + RUN - 1
    own = (k_ref, v_ref)

    loads = (
        pltpu.make_async_copy(q_hbm, q_ref, ws.at[0]),
        pltpu.make_async_copy(do_hbm, do_ref, ws.at[1]),
        pltpu.make_async_copy(wq_hbm, wq, ws.at[2]),
        pltpu.make_async_copy(wk_hbm, wkv.at[:, pl.ds(0, HD)], ws.at[3]),
        pltpu.make_async_copy(wv_hbm, wkv.at[:, pl.ds(HD, HD)], ws.at[4]),
    )
    for load in loads:
        load.start()
    greet(
        [("seq", n) for n in (zu, zd, yp, ym, y2)]
        + [("head", n) for n in (partner,) + xpeers]
    )

    def ring(up, t, kv):
        chunk = lax.rem(z + (NZ - t if up else t), NZ)
        where = tab.at[kv, rows_of(chunk * ROWS, ROWS)]
        i = 0 if up else 1
        return send(
            own[kv] if t == 0 else where, where, zs.at[i, t, kv], zr.at[i, t, kv],
            "seq", zu if up else zd,
        )

    def landed(up, t, kv):
        chunk = lax.rem(z + (NZ - 1 - t if up else 1 + t), NZ)
        where = tab.at[kv, rows_of(chunk * ROWS, ROWS)]
        i = 0 if up else 1
        return send(where, where, zs.at[i, t, kv], zr.at[i, t, kv], "seq", zu if up else zd)

    def slot_copy(p, chunk, kv):
        first = (FROM_DOWN, FROM_UP, FROM_FAR)[p]
        at = rows_of((first + chunk * 2) * BLOCK, 2 * BLOCK)
        return send(
            ysend.at[p, chunk, kv], tab.at[kv, at, :], ys.at[p, chunk, kv], yr.at[p, chunk, kv],
            "seq", ypeers[p],
        )

    def global_copy(p, kv):
        return send(
            tab.at[kv, pl.ds(0, 2 * BLOCK), :],
            tab.at[kv, pl.ds((EXTRA + 2) * BLOCK, 2 * BLOCK), :],
            gs.at[p, kv], gr.at[kv], "seq", ypeers[p],
        )

    def halo_copy(p, kv):
        if p == 0:
            row = lax.rem(z + NZ - lax.div(y, 3), NZ) * ROWS + (RUN - 1) * BLOCK
        else:
            row = lax.rem(z + lax.div(3 - y, 3), NZ) * ROWS
        at = pl.ds((EXTRA + p) * BLOCK, BLOCK)
        return send(
            tab.at[kv, rows_of(row, BLOCK), :], tab.at[kv, at, :], hs.at[p, kv], hr.at[p, kv],
            "seq", ypeers[p],
        )

    def spread(chunk, kv):
        stage[kv] = tab[kv, rows_of(chunk * ROWS, ROWS), :].reshape(RUN, BLOCK, HD)
        for p, rel in ((2, 2), (0, 1), (1, 3)):
            for k in range(2):
                pick = idx[k * OWNERS + chunk * NY + y, plane + lax.rem(y + rel, NY) * RUN]
                ysend[p, chunk, kv, k * BLOCK : (k + 1) * BLOCK, :] = stage[kv, pick]
        for p in (2, 0, 1):
            slot_copy(p, chunk, kv).start()

        @pl.when(jnp.logical_and(chunk == 0, y == 0))
        def _():
            for p in range(3):
                global_copy(p, kv).start()

    for kv in range(2):
        ring(True, 0, kv).start()
        ring(False, 0, kv).start()
    index_tables(owner_ref, block_ref, tables, z, y)
    to_scalar = pltpu.make_async_copy(tables, idx, ts)
    to_scalar.start()
    for kv in range(2):
        tab[kv, rows_of(z * ROWS, ROWS), :] = own[kv][...]
    to_scalar.wait()
    for kv in range(2):
        spread(z, kv)
    for t in range(4):
        for kv in range(2):
            ups = (True, False) if t < 3 else ((True,) if kv == 0 else (False,))
            for up in ups:
                landed(up, t, kv).wait_recv()
                if t < 2 or (t == 2 and kv == (0 if up else 1)):
                    ring(up, t + 1, kv).start()
            for up in ups:
                spread(lax.rem(z + (NZ - 1 - t if up else 1 + t), NZ), kv)
            if t == 0:
                for p in range(2):
                    halo_copy(p, kv).start()

    loads[0].wait()
    loads[1].wait()
    wacc[...] = jnp.zeros_like(wacc)
    gacc[...] = jnp.zeros_like(gacc)
    for kv in range(2):
        for p in range(3):
            for n in range(NZ):
                slot_copy(p, n, kv).wait_recv()
        for p in range(2):
            halo_copy(p, kv).wait_recv()

        @pl.when(y == 0)
        def _():
            tab[kv, (EXTRA + 2) * BLOCK : (EXTRA + 4) * BLOCK, :] = tab[kv, 0 : 2 * BLOCK, :]

        @pl.when(y != 0)
        def _():
            global_copy(0, kv).wait_recv()

    def attend(step, carry):
        grads = []
        for n in range(PER):
            b = step * PER + n
            index = [
                jnp.where(b == 0, EXTRA, z * RUN + b - 1),
                z * RUN + b,
                jnp.where(b == RUN - 1, EXTRA + 1, z * RUN + b + 1),
                EXTRA + 2,
                EXTRA + 3,
            ] + [idx[LISTS + j, plane - (RUN - 1) + y * RUN + b] for j in range(3)]
            for j in range(8):
                at = index[j]
                kl[n, j * BLOCK : (j + 1) * BLOCK, :] = tab_blocks[0, at]
                vl[n, j * BLOCK : (j + 1) * BLOCK, :] = tab_blocks[1, at]
        for n in range(PER):
            b = step * PER + n
            mine = rows_of(b * BLOCK, BLOCK)
            q4 = jnp.concatenate([q_ref[mine, g * HD : (g + 1) * HD] for g in range(GROUP)], axis=0)
            d4 = jnp.concatenate([do_ref[mine, g * HD : (g + 1) * HD] for g in range(GROUP)], axis=0)
            keys = kl[n]
            vals = vl[n]
            scores = dot(keys, q4, NT)
            no_left = jnp.logical_and(s == 0, b == 0)
            no_right = jnp.logical_and(s == NZ * NY - 1, b == RUN - 1)
            scores = jnp.concatenate(
                [
                    jnp.where(no_left, -1e30, scores[:BLOCK]),
                    scores[BLOCK : 2 * BLOCK],
                    jnp.where(no_right, -1e30, scores[2 * BLOCK : 3 * BLOCK]),
                    scores[3 * BLOCK :],
                ],
                axis=0,
            )
            row_max = jnp.max(scores, axis=0, keepdims=True)
            powers = jnp.exp((scores - row_max) * SCALE)
            weights = powers * (1.0 / jnp.sum(powers, axis=0, keepdims=True))
            weights_half = weights.astype(jnp.bfloat16)
            dprob = dot(vals, d4, NT)
            delta = jnp.sum(weights_half.astype(jnp.float32) * dprob, axis=0, keepdims=True)
            dscore_half = (weights * (dprob - delta)).astype(jnp.bfloat16)
            dq = (dot(dscore_half, keys, TN) * SCALE).astype(jnp.bfloat16)
            for g in range(GROUP):
                dq_ref[mine, g * HD : (g + 1) * HD] = dq[g * BLOCK : (g + 1) * BLOCK]
            grads.append((dot(dscore_half, q4, NN) * SCALE, dot(weights_half, d4, NN)))
        for n in range(PER):
            b = step * PER + n
            for kv in range(2):
                grad = grads[n][kv]
                wacc[kv, rows_of(b * BLOCK, 3 * BLOCK), :] += grad[: 3 * BLOCK]
                gacc[kv] += grad[3 * BLOCK : 5 * BLOCK]
                for j in range(3):
                    rp[kv, b * 3 + j] = grad[(5 + j) * BLOCK : (6 + j) * BLOCK].astype(jnp.bfloat16)
        return carry

    tab_blocks = tab.reshape(2, TABLE, BLOCK, HD)
    lax.fori_loop(0, RUN // PER, attend, 0)
    for kv in range(2):
        halo[kv, :BLOCK, :] = wacc[kv, :BLOCK, :].astype(jnp.bfloat16)
        halo[kv, BLOCK:, :] = wacc[kv, BLOCK + ROWS :, :].astype(jnp.bfloat16)
        glob[kv] = gacc[kv].astype(jnp.bfloat16)

    def back_copy(p, chunk, kv):
        return send(
            rsend.at[p, chunk, kv], ybuf.at[p, chunk, kv], ys2.at[p, chunk, kv],
            yr2.at[p, chunk, kv], "seq", ypeers[p],
        )

    def halo_back(p):
        half = pl.ds(BLOCK if p == 0 else 0, BLOCK)
        return send(halo.at[:, half, :], hbuf.at[p], hs2.at[p], hr2.at[p], "seq", ypeers[p])

    def global_back(slot):
        return send(glob, gbuf.at[slot], gs2, gr2.at[slot], "seq", z * NY)

    events = [(4, 0, 0), (4, 1, 1)]
    for m in (3, 2, 1):
        events += [(m, 1, 0), (-m, 0, 1), (m, 0, 0), (-m, 1, 1)]
    events += [(0, 0, None), (0, 1, None)]
    low_chunk = lax.rem(z + NZ - lax.div(y, 3), NZ)
    high_chunk = lax.rem(z + lax.div(3 - y, 3), NZ)

    def entry_of(k, chunk, rel):
        return idx[ENTRY + k * OWNERS + chunk * NY + lax.rem(y + rel, NY), plane + y * RUN]

    def offer(event):
        off, kv, _ = event
        chunk = lax.rem(z + off + NZ, NZ)
        for p, rel in ((2, 2), (0, 1), (1, 3)):
            for k in range(2):
                rsend[p, chunk, kv, k * BLOCK : (k + 1) * BLOCK, :] = rp[kv, entry_of(k, chunk, rel)]
        for p in (2, 0, 1):
            back_copy(p, chunk, kv).start()

    def collect(event):
        off, kv, _ = event
        chunk = lax.rem(z + off + NZ, NZ)
        for p in range(3):
            back_copy(p, chunk, kv).wait_recv()
        data = []
        picks = []
        for k in range(2):
            data.append(rp[kv, entry_of(k, chunk, 0)].astype(jnp.float32))
            for p in range(3):
                data.append(
                    ybuf[p, chunk, kv, k * BLOCK : (k + 1) * BLOCK, :].astype(jnp.float32)
                )
            for rel in (0, 3, 1, 2):
                picks.append(
                    idx[RAW + k * OWNERS + chunk * NY + y, plane + lax.rem(y + rel, NY) * RUN]
                )

        def one(b, carry):
            total = jnp.where(picks[0] == b, data[0], 0.0)
            for i in range(1, 8):
                total = total + jnp.where(picks[i] == b, data[i], 0.0)
            acc[kv, rows_of(b * BLOCK, BLOCK), :] = total
            return carry

        lax.fori_loop(0, RUN, one, 0)

        @pl.when(chunk == low_chunk)
        def _():
            acc[kv, (RUN - 1) * BLOCK :, :] += hbuf[1, kv].astype(jnp.float32)

        @pl.when(chunk == high_chunk)
        def _():
            acc[kv, :BLOCK, :] += hbuf[0, kv].astype(jnp.float32)

        @pl.when(jnp.logical_and(chunk == 0, y == 0))
        def _():
            total = glob[kv].astype(jnp.float32)
            for m in range(3):
                total = total + gbuf[m, kv].astype(jnp.float32)
            acc[kv, 0 : 2 * BLOCK, :] += total

    bufs = (zup, zdown)
    zpeer = (zu, zd)

    def zring(i, t, kv):
        return send(
            bufs[i].at[0, t, kv], bufs[i].at[1, t, kv], zs2.at[i, t, kv], zr2.at[i, t, kv],
            "seq", zpeer[i],
        )

    def zpush(event):
        off, kv, i = event
        t = 4 - abs(off)
        total = acc[kv]
        if t >= 2 or (t == 1 and kv == i):
            zring(i, t - 1, kv).wait_recv()
            total = total + bufs[i][1, t - 1, kv].astype(jnp.float32)
        bufs[i][0, t, kv] = total.astype(jnp.bfloat16)
        zring(i, t, kv).start()

    def token_rows(d):
        return rows_of(lax.rem(x + d, NX) * 2 * BLOCK, 2 * BLOCK)

    def query_part(n):
        d = (2, 1, 3, 0)[n // 2]
        a = dq_ref[token_rows(d), :]

        def tile(m, carry):
            w = pl.ds(pl.multiple_of(m * TILE, TILE), TILE)
            total_ref[d, :, w] = dot(a, wq[w, :], NT)
            return carry

        half = D // TILE // 2
        lax.fori_loop(n % 2 * half, n % 2 * half + half, tile, 0)

    halo_back(0).start()
    halo_back(1).start()
    for n in range(1, NY):
        @pl.when(y == n)
        def _():
            global_back(n - 1).start()
    ahead = 6
    for event in events[:ahead]:
        offer(event)
    for load in loads[2:]:
        load.wait()
    query_part(0)
    query_part(1)
    for p in range(2):
        halo_back(p).wait_recv()

    @pl.when(y == 0)
    def _():
        for m in range(3):
            global_back(m).wait_recv()

    parts = 2
    for n, event in enumerate(events[:14]):
        collect(event)
        zpush(event)
        if n + ahead < 16:
            offer(events[n + ahead])
        if n % 2 == 1 and parts < 8:
            query_part(parts)
            parts += 1
    for kv in range(2):
        collect(events[14 + kv])
    for kv in range(2):
        total = acc[kv] + wacc[kv, BLOCK : BLOCK + ROWS, :]
        for i in range(2):
            zring(i, 3, kv).wait_recv()
            total = total + bufs[i][1, 3, kv].astype(jnp.float32)
        dkv[:, kv * HD : (kv + 1) * HD] = total.astype(jnp.bfloat16)

    def cols(quarter):
        return pl.ds(quarter * QUARTER, QUARTER)

    def pair_copy(d, quarter):
        return send(
            term.at[d, rows_of((1 - c) * BLOCK, BLOCK), cols(quarter)],
            pair.at[d, :, cols(quarter)], ps.at[d, quarter], pr.at[d, quarter],
            "head", partner,
        )

    def xring(i, t, quarter):
        return send(
            xout.at[i, t, :, cols(quarter)], xin.at[i, t, :, cols(quarter)],
            xs.at[i, t, quarter], xr.at[i, t, quarter], "head", xpeers[i],
        )

    def compute(d):
        a = dkv[token_rows(d), :]
        for quarter in range(4):
            def tile(n, carry):
                w = pl.ds(pl.multiple_of(quarter * QUARTER + n * TILE, TILE), TILE)
                total = total_ref[d, :, w] + dot(a, wkv[w, :], NT)
                term[d, :, w] = total.astype(jnp.bfloat16)
                return carry

            lax.fori_loop(0, QUARTER // TILE, tile, 0)
            pair_copy(d, quarter).start()

    def both(d, quarter):
        pair_copy(d, quarter).wait_recv()
        mine = term[d, rows_of(c * BLOCK, BLOCK), cols(quarter)].astype(jnp.float32)
        return mine + pair[d, :, cols(quarter)].astype(jnp.float32)

    def arrived(i, t, quarter):
        xring(i, t, quarter).wait_recv()
        return xin[i, t, :, cols(quarter)].astype(jnp.float32)

    def xpush(i, t, quarter, total):
        xout[i, t, :, cols(quarter)] = total.astype(jnp.bfloat16)
        xring(i, t, quarter).start()

    compute(2)
    compute(1)
    for n in range(2):
        xpush(0, 0, n, both(2, n))
        xpush(1, 0, 2 + n, both(2, 2 + n))
    compute(3)
    for n in range(2):
        xpush(0, 1, 2 + n, both(1, 2 + n))
        xpush(1, 1, n, both(3, n))
    compute(0)
    for n in range(2):
        xpush(0, 1, n, both(1, n) + arrived(0, 0, n))
        xpush(1, 1, 2 + n, both(3, 2 + n) + arrived(1, 0, 2 + n))
    for quarter in (2, 3, 0, 1):
        total = both(0, quarter) + arrived(0, 1, quarter) + arrived(1, 1, quarter)
        out[:, cols(quarter)] = total.astype(jnp.bfloat16)

    for i in range(2):
        for t in range(4):
            for kv in range(2):
                if t < 3 or kv == i:
                    ring(i == 0, t, kv).wait_send()
                if t > 0 or kv == i:
                    zring(i, t, kv).wait_send()
    for p in range(3):
        for n in range(NZ):
            for kv in range(2):
                slot_copy(p, n, kv).wait_send()
                back_copy(p, n, kv).wait_send()
    for p in range(2):
        for kv in range(2):
            halo_copy(p, kv).wait_send()
        halo_back(p).wait_send()

    @pl.when(y == 0)
    def _():
        for p in range(3):
            for kv in range(2):
                global_copy(p, kv).wait_send()

    @pl.when(y != 0)
    def _():
        global_back(0).wait_send()

    for d in range(4):
        for quarter in range(4):
            pair_copy(d, quarter).wait_send()
    for i in range(2):
        for quarter in range(4):
            if quarter // 2 == i:
                xring(i, 0, quarter).wait_send()
            xring(i, 1, quarter).wait_send()


def whole(owners, blocks, keys, values, query, grad_out, wq, wk, wv):
    anywhere = pl.BlockSpec(memory_space=pl.ANY)
    half = jnp.bfloat16
    full = jnp.float32
    slots = (3, NZ, 2, 2 * BLOCK, HD)
    return pl.pallas_call(
        whole_kernel,
        out_shape=sds((BLOCK, D)),
        in_specs=[vmem()] * 4 + [anywhere] * 5,
        out_specs=vmem(),
        scratch_shapes=[
            VM((LISTS + 8, 128), jnp.int32),
            pltpu.SMEM((LISTS + 8, 128), jnp.int32),
            VM((2, TABLE * BLOCK, HD), half),
            VM((2, RUN, BLOCK, HD), half),
            VM(slots, half),
            VM((ROWS, GROUP * HD), half),
            VM((ROWS, GROUP * HD), half),
            VM((ROWS, GROUP * HD), half),
            VM((PER, ROWS, HD), half),
            VM((PER, ROWS, HD), half),
            VM((2, ROWS + 2 * BLOCK, HD), full),
            VM((2, 2 * BLOCK, HD), full),
            VM((2, RUN * 3, BLOCK, HD), half),
            VM((2, 2 * BLOCK, HD), half),
            VM((2, 2 * BLOCK, HD), half),
            VM((D, GROUP * HD), half),
            VM((D, 2 * HD), half),
            VM((ROWS, 2 * HD), half),
            VM(slots, half),
            VM(slots, half),
            VM((2, 2, BLOCK, HD), half),
            VM((3, 2, 2 * BLOCK, HD), half),
            VM((2, ROWS, HD), full),
            VM((2, 4, 2, ROWS, HD), half),
            VM((2, 4, 2, ROWS, HD), half),
            VM((4, 2 * BLOCK, D), full),
            VM((4, 2 * BLOCK, D), half),
            VM((4, BLOCK, D), half),
            VM((2, 2, BLOCK, D), half),
            VM((2, 2, BLOCK, D), half),
            DMA,
            DMA((5,)),
            DMA((2, 4, 2)),
            DMA((2, 4, 2)),
            DMA((3, NZ, 2)),
            DMA((3, NZ, 2)),
            DMA((2, 2)),
            DMA((2, 2)),
            DMA((3, 2)),
            DMA((2,)),
            DMA((2, 4, 2)),
            DMA((2, 4, 2)),
            DMA((3, NZ, 2)),
            DMA((3, NZ, 2)),
            DMA((2,)),
            DMA((2,)),
            DMA,
            DMA((3,)),
            DMA((4, 4)),
            DMA((4, 4)),
            DMA((2, 2, 4)),
            DMA((2, 2, 4)),
        ],
        compiler_params=pltpu.CompilerParams(
            collective_id=0, has_side_effects=True, vmem_limit_bytes=60 * 2**20
        ),
        name="whole",
    )(owners, blocks, keys, values, query, grad_out, wq, wk, wv)


def on_device(query, keys, values, grad_out, w_query, w_key, w_value, rand_owner, rand_block):
    return whole(
        rand_owner.T, rand_block.T, keys, values, query, grad_out, w_query, w_key, w_value
    )


def solution(mesh):
    return jax.shard_map(
        on_device,
        mesh=mesh,
        in_specs=(
            P("seq", "head"),
            P("seq", "head"),
            P("seq", "head"),
            P("seq", "head"),
            P(None, "head"),
            P(None, "head"),
            P(None, "head"),
            P(),
            P(),
        ),
        out_specs=P(("seq", "head"), None),
        check_vma=False,
    )
```

```python
import functools

import jax
import jax.numpy as jnp
from jax import lax
from jax.experimental import pallas as pl
from jax.experimental.pallas import tpu as pltpu
from jax.sharding import PartitionSpec as P

BLOCK = 64
HD = 128
NZ = 8
NY = 4
NX = 4
RUN = 8
ROWS = RUN * BLOCK
HALF = ROWS // 2
GROUP = 4
D = 4096
FROM_UP = NZ * RUN
FROM_DOWN = FROM_UP + 2 * NZ
FROM_FAR = FROM_DOWN + 2 * NZ
EXTRA = FROM_FAR + 2 * NZ
TABLE = EXTRA + 4
OWNERS = NZ * NY
RAW = 2 * OWNERS
ENTRY = 4 * OWNERS
LISTS = 6 * OWNERS
QUARTER = D // 4
TILE = 512
PER = 2
MESH = pl.DeviceIdType.MESH
SCALE = HD ** (-0.5)
VM = pltpu.VMEM
DMA = pltpu.SemaphoreType.DMA
NT = (((1,), (1,)), ((), ()))
NN = (((1,), (0,)), ((), ()))
TN = (((0,), (0,)), ((), ()))


def vmem():
    return pl.BlockSpec(memory_space=pltpu.VMEM)


def sds(shape, dtype=jnp.bfloat16):
    return jax.ShapeDtypeStruct(shape, dtype)


def dot(a, b, dims):
    return lax.dot_general(a, b, dims, preferred_element_type=jnp.float32)


def seq_place():
    s = lax.axis_index("seq")
    return s, lax.div(s, NY), lax.rem(s, NY)


def rows_of(start, size):
    return pl.ds(pl.multiple_of(start, BLOCK), size)


def neighbours(z, y):
    return (
        lax.rem(z + 1, NZ) * NY + y,
        lax.rem(z + NZ - 1, NZ) * NY + y,
        z * NY + lax.rem(y + 1, NY),
        z * NY + lax.rem(y + 3, NY),
        z * NY + lax.rem(y + 2, NY),
    )


def greet(peers):
    barrier = pltpu.get_barrier_semaphore()
    for axis, peer in peers:
        pl.semaphore_signal(barrier, inc=1, device_id={axis: peer}, device_id_type=MESH)
    pl.semaphore_wait(barrier, len(peers))


def send(src, dst, ssem, rsem, axis, peer):
    return pltpu.make_async_remote_copy(
        src_ref=src,
        dst_ref=dst,
        send_sem=ssem,
        recv_sem=rsem,
        device_id={axis: peer},
        device_id_type=MESH,
    )


def group_prefix(value, lane):
    for shift in (1, 2, 4):
        value = value + jnp.where(lane >= shift, pltpu.roll(value, shift, 1), 0)
    return value


def index_tables(owner_ref, block_ref, out, z, y):
    low = z < NZ // 2
    owners = jnp.where(low, owner_ref[:, :128], owner_ref[:, 128:])
    picks = jnp.where(low, block_ref[:, :128], block_ref[:, 128:])
    shape = (OWNERS, 128)
    index = lax.broadcasted_iota(jnp.int32, shape, 0)
    lane = lax.broadcasted_iota(jnp.int32, shape, 1) & 7
    hits = [jnp.broadcast_to(owners[j : j + 1], shape) == index for j in range(3)]
    named = jnp.zeros(shape, jnp.int32)
    chosen = jnp.zeros(shape, jnp.int32)
    entry = lane * 3
    for j in range(3):
        named = named + jnp.where(hits[j], 1, 0)
        chosen = chosen + jnp.where(hits[j], jnp.broadcast_to(picks[j : j + 1], shape), 0)
        entry = entry + jnp.where(hits[j], j, 0)
    place = group_prefix(named, lane) - named
    for k in range(2):
        mine = (named == 1) & (place == k)
        pick = group_prefix(jnp.where(mine, chosen + 1, 0), lane) - 1
        out[k * OWNERS : (k + 1) * OWNERS, :] = jnp.maximum(pick, 0)
        out[RAW + k * OWNERS : RAW + (k + 1) * OWNERS, :] = pick
        out[ENTRY + k * OWNERS : ENTRY + (k + 1) * OWNERS, :] = group_prefix(
            jnp.where(mine, entry, 0), lane
        )
    for j in range(3):
        owner = owners[j : j + 1]
        at = jnp.minimum(jnp.sum(jnp.where(hits[j], place, 0), axis=0, keepdims=True), 1)
        zo = owner >> 2
        rel = ((owner & 3) - y + NY) & 3
        first = jnp.where(rel == 1, FROM_UP, jnp.where(rel == 2, FROM_FAR, FROM_DOWN))
        out[LISTS + j : LISTS + j + 1, :] = jnp.where(
            rel == 0, zo * RUN + picks[j : j + 1], first + zo * 2 + at
        )


def whole_kernel(
    owner_hbm, block_hbm, k_ref, v_ref, q_hbm, do_hbm, wq_hbm, wk_hbm, wv_hbm, out,
    owner_ref, block_ref, tables, idx, tab, stage, ysend, q_ref, do_ref, dq_ref, kl, vl, wacc, gacc, rp,
    halo, glob, wq, wkv, dkv, rsend, ybuf, hbuf, gbuf, pickers, acc, zup, zdown,
    total_ref, term, pair, xout, xin,
    ts, ws, zs, zr, ys, yr, hs, hr, gs, gr,
    zs2, zr2, ys2, yr2, hs2, hr2, gs2, gr2, ps, pr, xs, xr
):
    s, z, y = seq_place()
    zu, zd, yp, ym, y2 = neighbours(z, y)
    ypeers = (yp, ym, y2)
    h = lax.axis_index("head")
    x = lax.div(h, 2)
    c = lax.rem(h, 2)
    partner = x * 2 + 1 - c
    xpeers = (lax.rem(x + 1, NX) * 2 + c, lax.rem(x + NX - 1, NX) * 2 + c)
    plane = lax.rem(z, NZ // 2) * (NY * RUN) + RUN - 1
    own = (k_ref, v_ref)

    loads = (
        pltpu.make_async_copy(q_hbm, q_ref, ws.at[0]),
        pltpu.make_async_copy(do_hbm, do_ref, ws.at[1]),
        pltpu.make_async_copy(wq_hbm, wq, ws.at[2]),
        pltpu.make_async_copy(wk_hbm, wkv.at[:, pl.ds(0, HD)], ws.at[3]),
        pltpu.make_async_copy(wv_hbm, wkv.at[:, pl.ds(HD, HD)], ws.at[4]),
    )
    mine = rows_of(z * ROWS, ROWS)
    first = (
        pltpu.make_async_copy(owner_hbm, owner_ref, ws.at[5]),
        pltpu.make_async_copy(block_hbm, block_ref, ws.at[6]),
        pltpu.make_async_copy(k_ref, tab.at[0, mine], ws.at[7]),
        pltpu.make_async_copy(v_ref, tab.at[1, mine], ws.at[8]),
    )
    for load in first:
        load.start()
    greet(
        [("seq", n) for n in (zu, zd, yp, ym, y2)]
        + [("head", n) for n in (partner,) + xpeers]
    )

    def ring(up, t, kv, half):
        chunk = lax.rem(z + (NZ - t if up else t), NZ)
        where = tab.at[kv, rows_of(chunk * ROWS + half * HALF, HALF)]
        i = 0 if up else 1
        n = kv * 2 + half
        return send(
            own[kv].at[pl.ds(half * HALF, HALF)] if t == 0 else where, where,
            zs.at[i, t, n], zr.at[i, t, n], "seq", zu if up else zd,
        )

    def landed(up, t, kv, half):
        chunk = lax.rem(z + (NZ - 1 - t if up else 1 + t), NZ)
        where = tab.at[kv, rows_of(chunk * ROWS + half * HALF, HALF)]
        i = 0 if up else 1
        n = kv * 2 + half
        return send(where, where, zs.at[i, t, n], zr.at[i, t, n], "seq", zu if up else zd)

    def slot_copy(p, chunk, kv):
        first = (FROM_DOWN, FROM_UP, FROM_FAR)[p]
        at = rows_of((first + chunk * 2) * BLOCK, 2 * BLOCK)
        return send(
            ysend.at[p, chunk, kv], tab.at[kv, at, :], ys.at[p, chunk, kv], yr.at[p, chunk, kv],
            "seq", ypeers[p],
        )

    def global_copy(p, kv):
        return send(
            tab.at[kv, pl.ds(0, 2 * BLOCK), :],
            tab.at[kv, pl.ds((EXTRA + 2) * BLOCK, 2 * BLOCK), :],
            gs.at[p, kv], gr.at[kv], "seq", ypeers[p],
        )

    def halo_copy(p, kv):
        if p == 0:
            row = lax.rem(z + NZ - lax.div(y, 3), NZ) * ROWS + (RUN - 1) * BLOCK
        else:
            row = lax.rem(z + lax.div(3 - y, 3), NZ) * ROWS
        at = pl.ds((EXTRA + p) * BLOCK, BLOCK)
        return send(
            tab.at[kv, rows_of(row, BLOCK), :], tab.at[kv, at, :], hs.at[p, kv], hr.at[p, kv],
            "seq", ypeers[p],
        )

    def spread(chunk, kv):
        stage[kv] = tab[kv, rows_of(chunk * ROWS, ROWS), :].reshape(RUN, BLOCK, HD)
        for p, rel in ((2, 2), (0, 1), (1, 3)):
            for k in range(2):
                pick = idx[k * OWNERS + chunk * NY + y, plane + lax.rem(y + rel, NY) * RUN]
                ysend[p, chunk, kv, k * BLOCK : (k + 1) * BLOCK, :] = stage[kv, pick]
        for p in (2, 0, 1):
            slot_copy(p, chunk, kv).start()

        @pl.when(jnp.logical_and(chunk == 0, y == 0))
        def _():
            for p in range(3):
                global_copy(p, kv).start()

    for kv in range(2):
        for half in range(2):
            ring(True, 0, kv, half).start()
            ring(False, 0, kv, half).start()
    first[0].wait()
    first[1].wait()
    index_tables(owner_ref, block_ref, tables, z, y)
    to_scalar = pltpu.make_async_copy(tables, idx, ts)
    to_scalar.start()
    first[2].wait()
    first[3].wait()
    to_scalar.wait()
    for kv in range(2):
        spread(z, kv)
    for load in loads:
        load.start()
    for t in range(4):
        for kv in range(2):
            ups = (True, False) if t < 3 else ((True,) if kv == 0 else (False,))
            for half in range(2):
                for up in ups:
                    landed(up, t, kv, half).wait_recv()
                    if t < 2 or (t == 2 and kv == (0 if up else 1)):
                        ring(up, t + 1, kv, half).start()
            for up in ups:
                spread(lax.rem(z + (NZ - 1 - t if up else 1 + t), NZ), kv)
            if t == 0:
                for p in range(2):
                    halo_copy(p, kv).start()

    loads[0].wait()
    loads[1].wait()
    wacc[...] = jnp.zeros_like(wacc)
    gacc[...] = jnp.zeros_like(gacc)
    for kv in range(2):
        for p in range(3):
            for n in range(NZ):
                slot_copy(p, n, kv).wait_recv()
        for p in range(2):
            halo_copy(p, kv).wait_recv()

        @pl.when(y == 0)
        def _():
            tab[kv, (EXTRA + 2) * BLOCK : (EXTRA + 4) * BLOCK, :] = tab[kv, 0 : 2 * BLOCK, :]

        @pl.when(y != 0)
        def _():
            global_copy(0, kv).wait_recv()

    def attend(step, carry):
        grads = []
        for n in range(PER):
            b = step * PER + n
            index = [
                jnp.where(b == 0, EXTRA, z * RUN + b - 1),
                z * RUN + b,
                jnp.where(b == RUN - 1, EXTRA + 1, z * RUN + b + 1),
                EXTRA + 2,
                EXTRA + 3,
            ] + [idx[LISTS + j, plane - (RUN - 1) + y * RUN + b] for j in range(3)]
            for j in range(8):
                at = index[j]
                kl[n, j * BLOCK : (j + 1) * BLOCK, :] = tab_blocks[0, at]
                vl[n, j * BLOCK : (j + 1) * BLOCK, :] = tab_blocks[1, at]
        for n in range(PER):
            b = step * PER + n
            mine = rows_of(b * BLOCK, BLOCK)
            q4 = jnp.concatenate([q_ref[mine, g * HD : (g + 1) * HD] for g in range(GROUP)], axis=0)
            d4 = jnp.concatenate([do_ref[mine, g * HD : (g + 1) * HD] for g in range(GROUP)], axis=0)
            keys = kl[n]
            vals = vl[n]
            scores = dot(keys, q4, NT)
            no_left = jnp.logical_and(s == 0, b == 0)
            no_right = jnp.logical_and(s == NZ * NY - 1, b == RUN - 1)
            scores = jnp.concatenate(
                [
                    jnp.where(no_left, -1e30, scores[:BLOCK]),
                    scores[BLOCK : 2 * BLOCK],
                    jnp.where(no_right, -1e30, scores[2 * BLOCK : 3 * BLOCK]),
                    scores[3 * BLOCK :],
                ],
                axis=0,
            )
            row_max = jnp.max(scores, axis=0, keepdims=True)
            powers = jnp.exp((scores - row_max) * SCALE)
            weights = powers * (1.0 / jnp.sum(powers, axis=0, keepdims=True))
            weights_half = weights.astype(jnp.bfloat16)
            dprob = dot(vals, d4, NT)
            delta = jnp.sum(weights_half.astype(jnp.float32) * dprob, axis=0, keepdims=True)
            dscore_half = (weights * (dprob - delta)).astype(jnp.bfloat16)
            dq = (dot(dscore_half, keys, TN) * SCALE).astype(jnp.bfloat16)
            for g in range(GROUP):
                dq_ref[mine, g * HD : (g + 1) * HD] = dq[g * BLOCK : (g + 1) * BLOCK]
            grads.append((dot(dscore_half, q4, NN) * SCALE, dot(weights_half, d4, NN)))
        for n in range(PER):
            b = step * PER + n
            for kv in range(2):
                grad = grads[n][kv]
                wacc[kv, rows_of(b * BLOCK, 3 * BLOCK), :] += grad[: 3 * BLOCK]
                gacc[kv] += grad[3 * BLOCK : 5 * BLOCK]
                for j in range(3):
                    rp[kv, b * 3 + j] = grad[(5 + j) * BLOCK : (6 + j) * BLOCK].astype(jnp.bfloat16)
        return carry

    tab_blocks = tab.reshape(2, TABLE, BLOCK, HD)
    lax.fori_loop(0, RUN // PER, attend, 0)
    for kv in range(2):
        halo[kv, :BLOCK, :] = wacc[kv, :BLOCK, :].astype(jnp.bfloat16)
        halo[kv, BLOCK:, :] = wacc[kv, BLOCK + ROWS :, :].astype(jnp.bfloat16)
        glob[kv] = gacc[kv].astype(jnp.bfloat16)

    def back_copy(p, chunk, kv):
        return send(
            rsend.at[p, chunk, kv], ybuf.at[p, chunk, kv], ys2.at[p, chunk, kv],
            yr2.at[p, chunk, kv], "seq", ypeers[p],
        )

    def halo_back(p, kv):
        half = pl.ds(BLOCK if p == 0 else 0, BLOCK)
        return send(
            halo.at[kv, half, :], hbuf.at[p, kv], hs2.at[p, kv], hr2.at[p, kv],
            "seq", ypeers[p],
        )

    def global_back(slot, kv):
        return send(glob.at[kv], gbuf.at[slot, kv], gs2.at[kv], gr2.at[slot, kv], "seq", z * NY)

    events = [(4, 0, 0), (4, 1, 1)]
    for m in (3, 2, 1):
        events += [(m, 1, 0), (-m, 0, 1), (m, 0, 0), (-m, 1, 1)]
    events += [(0, 0, None), (0, 1, None)]
    low_chunk = lax.rem(z + NZ - lax.div(y, 3), NZ)
    high_chunk = lax.rem(z + lax.div(3 - y, 3), NZ)

    def entry_of(k, chunk, rel):
        return idx[ENTRY + k * OWNERS + chunk * NY + lax.rem(y + rel, NY), plane + y * RUN]

    def offer(event):
        off, kv, _ = event
        chunk = lax.rem(z + off + NZ, NZ)
        for p, rel in ((2, 2), (0, 1), (1, 3)):
            for k in range(2):
                rsend[p, chunk, kv, k * BLOCK : (k + 1) * BLOCK, :] = rp[kv, entry_of(k, chunk, rel)]
        for p in (2, 0, 1):
            back_copy(p, chunk, kv).start()

    done = []

    def collect(event):
        off, kv, _ = event
        chunk = lax.rem(z + off + NZ, NZ)
        for p in range(3):
            back_copy(p, chunk, kv).wait_recv()
        slot = 1 if off < 0 else 0
        if (off, 1 - kv) not in done:
            lane = lax.broadcasted_iota(jnp.int32, (1, HD), 1)
            row = lax.broadcasted_iota(jnp.int32, (ROWS, HD), 0)
            for n, rel in enumerate((0, 3, 1, 2)):
                first, second = [
                    idx[RAW + k * OWNERS + chunk * NY + y, plane + lax.rem(y + rel, NY) * RUN]
                    for k in range(2)
                ]
                target = jnp.where(lane < BLOCK, first, second) * BLOCK + (lane & (BLOCK - 1))
                pickers[slot, :, n * HD : (n + 1) * HD] = jnp.where(
                    row == target, 1.0, 0.0
                ).astype(jnp.bfloat16)
        done.append((off, kv))
        data = [rp[kv, entry_of(k, chunk, 0)] for k in range(2)]
        data += [ybuf[p, chunk, kv] for p in range(3)]
        acc[kv] = dot(pickers[slot], jnp.concatenate(data, axis=0), NN)

        @pl.when(chunk == low_chunk)
        def _():
            halo_back(1, kv).wait_recv()
            acc[kv, (RUN - 1) * BLOCK :, :] += hbuf[1, kv].astype(jnp.float32)

        @pl.when(chunk == high_chunk)
        def _():
            halo_back(0, kv).wait_recv()
            acc[kv, :BLOCK, :] += hbuf[0, kv].astype(jnp.float32)

        @pl.when(jnp.logical_and(chunk == 0, y == 0))
        def _():
            total = glob[kv].astype(jnp.float32)
            for m in range(3):
                global_back(m, kv).wait_recv()
                total = total + gbuf[m, kv].astype(jnp.float32)
            acc[kv, 0 : 2 * BLOCK, :] += total

    bufs = (zup, zdown)
    zpeer = (zu, zd)

    def zring(i, t, kv, n):
        at = pl.ds(n * HALF, HALF) if t < 3 else token_rows(n)
        return send(
            bufs[i].at[0, t, kv, at], bufs[i].at[1, t, kv, at], zs2.at[i, t, kv, n],
            zr2.at[i, t, kv, n], "seq", zpeer[i],
        )

    def zpush(event):
        off, kv, i = event
        t = 4 - abs(off)
        for half in range(2):
            at = pl.ds(half * HALF, HALF)
            total = acc[kv, at, :]
            if t >= 2 or (t == 1 and kv == i):
                zring(i, t - 1, kv, half).wait_recv()
                total = total + bufs[i][1, t - 1, kv, at, :].astype(jnp.float32)
            bufs[i][0, t, kv, at, :] = total.astype(jnp.bfloat16)
            if t < 3:
                zring(i, t, kv, half).start()
        if t == 3:
            for d in (2, 1, 3, 0):
                zring(i, t, kv, d).start()

    def token_rows(d):
        return rows_of(lax.rem(x + d, NX) * 2 * BLOCK, 2 * BLOCK)

    def query_part(n):
        d = (2, 1, 3, 0)[n // 2]
        a = dq_ref[token_rows(d), :]

        def tile(m, carry):
            w = pl.ds(pl.multiple_of(m * TILE, TILE), TILE)
            total_ref[d, :, w] = dot(a, wq[w, :], NT)
            return carry

        half = D // TILE // 2
        lax.fori_loop(n % 2 * half, n % 2 * half + half, tile, 0)

    ahead = 6
    for n, event in enumerate(events[:ahead]):
        if n < 2:
            for m in range(1, NY):
                @pl.when(y == m)
                def _():
                    global_back(m - 1, n).start()
        offer(event)
    for p in range(2):
        for kv in range(2):
            halo_back(p, kv).start()
    for load in loads[2:]:
        load.wait()
    query_part(0)
    query_part(1)

    parts = 2
    for n, event in enumerate(events[:14]):
        collect(event)
        zpush(event)
        if n + ahead < 16:
            offer(events[n + ahead])
        if n % 2 == 1 and parts < 8:
            query_part(parts)
            parts += 1
    for kv in range(2):
        collect(events[14 + kv])

    def settle(d):
        at = token_rows(d)
        shifted = rows_of(lax.rem(x + d, NX) * 2 * BLOCK + BLOCK, 2 * BLOCK)
        for kv in range(2):
            total = acc[kv, at, :] + wacc[kv, shifted, :]
            for i in range(2):
                zring(i, 3, kv, d).wait_recv()
                total = total + bufs[i][1, 3, kv, at, :].astype(jnp.float32)
            dkv[at, kv * HD : (kv + 1) * HD] = total.astype(jnp.bfloat16)

    def cols(quarter):
        return pl.ds(quarter * QUARTER, QUARTER)

    def pair_copy(d, quarter):
        return send(
            term.at[d, rows_of((1 - c) * BLOCK, BLOCK), cols(quarter)],
            pair.at[d, :, cols(quarter)], ps.at[d, quarter], pr.at[d, quarter],
            "head", partner,
        )

    def xring(i, t, quarter):
        return send(
            xout.at[i, t, :, cols(quarter)], xin.at[i, t, :, cols(quarter)],
            xs.at[i, t, quarter], xr.at[i, t, quarter], "head", xpeers[i],
        )

    def compute(d):
        settle(d)
        a = dkv[token_rows(d), :]
        for quarter in range(4):
            def tile(n, carry):
                w = pl.ds(pl.multiple_of(quarter * QUARTER + n * TILE, TILE), TILE)
                total = total_ref[d, :, w] + dot(a, wkv[w, :], NT)
                term[d, :, w] = total.astype(jnp.bfloat16)
                return carry

            lax.fori_loop(0, QUARTER // TILE, tile, 0)
            pair_copy(d, quarter).start()

    def both(d, quarter):
        pair_copy(d, quarter).wait_recv()
        mine = term[d, rows_of(c * BLOCK, BLOCK), cols(quarter)].astype(jnp.float32)
        return mine + pair[d, :, cols(quarter)].astype(jnp.float32)

    def arrived(i, t, quarter):
        xring(i, t, quarter).wait_recv()
        return xin[i, t, :, cols(quarter)].astype(jnp.float32)

    def xpush(i, t, quarter, total):
        xout[i, t, :, cols(quarter)] = total.astype(jnp.bfloat16)
        xring(i, t, quarter).start()

    compute(2)
    compute(1)
    for n in range(2):
        xpush(0, 0, n, both(2, n))
        xpush(1, 0, 2 + n, both(2, 2 + n))
    compute(3)
    for n in range(2):
        xpush(0, 1, 2 + n, both(1, 2 + n))
        xpush(1, 1, n, both(3, n))
    compute(0)
    for n in range(2):
        xpush(0, 1, n, both(1, n) + arrived(0, 0, n))
        xpush(1, 1, 2 + n, both(3, 2 + n) + arrived(1, 0, 2 + n))
    for quarter in (2, 3, 0, 1):
        total = both(0, quarter) + arrived(0, 1, quarter) + arrived(1, 1, quarter)
        out[:, cols(quarter)] = total.astype(jnp.bfloat16)

    for i in range(2):
        for t in range(4):
            for kv in range(2):
                for half in range(2):
                    if t < 3 or kv == i:
                        ring(i == 0, t, kv, half).wait_send()
                for n in range(2 if t < 3 else 4):
                    if t > 0 or kv == i:
                        zring(i, t, kv, n).wait_send()
    for p in range(3):
        for n in range(NZ):
            for kv in range(2):
                slot_copy(p, n, kv).wait_send()
                back_copy(p, n, kv).wait_send()
    for p in range(2):
        for kv in range(2):
            halo_copy(p, kv).wait_send()
            halo_back(p, kv).wait_send()

    @pl.when(y == 0)
    def _():
        for p in range(3):
            for kv in range(2):
                global_copy(p, kv).wait_send()

    @pl.when(y != 0)
    def _():
        for kv in range(2):
            global_back(0, kv).wait_send()

    for d in range(4):
        for quarter in range(4):
            pair_copy(d, quarter).wait_send()
    for i in range(2):
        for quarter in range(4):
            if quarter // 2 == i:
                xring(i, 0, quarter).wait_send()
            xring(i, 1, quarter).wait_send()


def whole(owners, blocks, keys, values, query, grad_out, wq, wk, wv):
    anywhere = pl.BlockSpec(memory_space=pltpu.HBM)
    half = jnp.bfloat16
    full = jnp.float32
    slots = (3, NZ, 2, 2 * BLOCK, HD)
    return pl.pallas_call(
        whole_kernel,
        out_shape=sds((BLOCK, D)),
        in_specs=[anywhere] * 9,
        out_specs=vmem(),
        scratch_shapes=[
            VM((3, OWNERS * RUN), jnp.int32),
            VM((3, OWNERS * RUN), jnp.int32),
            VM((LISTS + 8, 128), jnp.int32),
            pltpu.SMEM((LISTS + 8, 128), jnp.int32),
            VM((2, TABLE * BLOCK, HD), half),
            VM((2, RUN, BLOCK, HD), half),
            VM(slots, half),
            VM((ROWS, GROUP * HD), half),
            VM((ROWS, GROUP * HD), half),
            VM((ROWS, GROUP * HD), half),
            VM((PER, ROWS, HD), half),
            VM((PER, ROWS, HD), half),
            VM((2, ROWS + 2 * BLOCK, HD), full),
            VM((2, 2 * BLOCK, HD), full),
            VM((2, RUN * 3, BLOCK, HD), half),
            VM((2, 2 * BLOCK, HD), half),
            VM((2, 2 * BLOCK, HD), half),
            VM((D, GROUP * HD), half),
            VM((D, 2 * HD), half),
            VM((ROWS, 2 * HD), half),
            VM(slots, half),
            VM(slots, half),
            VM((2, 2, BLOCK, HD), half),
            VM((3, 2, 2 * BLOCK, HD), half),
            VM((2, ROWS, ROWS), half),
            VM((2, ROWS, HD), full),
            VM((2, 4, 2, ROWS, HD), half),
            VM((2, 4, 2, ROWS, HD), half),
            VM((4, 2 * BLOCK, D), full),
            VM((4, 2 * BLOCK, D), half),
            VM((4, BLOCK, D), half),
            VM((2, 2, BLOCK, D), half),
            VM((2, 2, BLOCK, D), half),
            DMA,
            DMA((9,)),
            DMA((2, 4, 4)),
            DMA((2, 4, 4)),
            DMA((3, NZ, 2)),
            DMA((3, NZ, 2)),
            DMA((2, 2)),
            DMA((2, 2)),
            DMA((3, 2)),
            DMA((2,)),
            DMA((2, 4, 2, 4)),
            DMA((2, 4, 2, 4)),
            DMA((3, NZ, 2)),
            DMA((3, NZ, 2)),
            DMA((2, 2)),
            DMA((2, 2)),
            DMA((2,)),
            DMA((3, 2)),
            DMA((4, 4)),
            DMA((4, 4)),
            DMA((2, 2, 4)),
            DMA((2, 2, 4)),
        ],
        compiler_params=pltpu.CompilerParams(
            collective_id=0, has_side_effects=True, vmem_limit_bytes=60 * 2**20
        ),
        name="whole",
    )(owners, blocks, keys, values, query, grad_out, wq, wk, wv)


def on_device(query, keys, values, grad_out, w_query, w_key, w_value, rand_owner, rand_block):
    return whole(
        rand_owner.T, rand_block.T, keys, values, query, grad_out, w_query, w_key, w_value
    )


def solution(mesh):
    return jax.shard_map(
        on_device,
        mesh=mesh,
        in_specs=(
            P("seq", "head"),
            P("seq", "head"),
            P("seq", "head"),
            P("seq", "head"),
            P(None, "head"),
            P(None, "head"),
            P(None, "head"),
            P(),
            P(),
        ),
        out_specs=P(("seq", "head"), None),
        check_vma=False,
    )
```

```python
import functools

import jax
import jax.numpy as jnp
from jax import lax
from jax.experimental import pallas as pl
from jax.experimental.pallas import tpu as pltpu
from jax.sharding import PartitionSpec as P

BLOCK = 64
HD = 128
NZ = 8
NY = 4
NX = 4
RUN = 8
ROWS = RUN * BLOCK
HALF = ROWS // 2
GROUP = 4
D = 4096
FROM_UP = NZ * RUN
FROM_DOWN = FROM_UP + 2 * NZ
FROM_FAR = FROM_DOWN + 2 * NZ
EXTRA = FROM_FAR + 2 * NZ
OPPOSITE = EXTRA + 4
TABLE = OPPOSITE + 2
OWNERS = NZ * NY
RAW = 2 * OWNERS
ENTRY = 4 * OWNERS
LISTS = 6 * OWNERS
FAR = LISTS + 8
FAR_RAW = FAR + 2 * OWNERS
INDEX_ROWS = FAR_RAW + 2 * OWNERS
NEAR = (0, 1, 2, 3, 5, 6, 7)
QUARTER = D // 4
TILE = 512
PER = 2
MESH = pl.DeviceIdType.MESH
SCALE = HD ** (-0.5)
VM = pltpu.VMEM
DMA = pltpu.SemaphoreType.DMA
NT = (((1,), (1,)), ((), ()))
NN = (((1,), (0,)), ((), ()))
TN = (((0,), (0,)), ((), ()))


def vmem():
    return pl.BlockSpec(memory_space=pltpu.VMEM)


def sds(shape, dtype=jnp.bfloat16):
    return jax.ShapeDtypeStruct(shape, dtype)


def dot(a, b, dims):
    return lax.dot_general(a, b, dims, preferred_element_type=jnp.float32)


def seq_place():
    s = lax.axis_index("seq")
    return s, lax.div(s, NY), lax.rem(s, NY)


def rows_of(start, size):
    return pl.ds(pl.multiple_of(start, BLOCK), size)


def neighbours(z, y):
    return (
        lax.rem(z + 1, NZ) * NY + y,
        lax.rem(z + NZ - 1, NZ) * NY + y,
        z * NY + lax.rem(y + 1, NY),
        z * NY + lax.rem(y + 3, NY),
        z * NY + lax.rem(y + 2, NY),
    )


def greet(peers):
    barrier = pltpu.get_barrier_semaphore()
    for axis, peer in peers:
        pl.semaphore_signal(barrier, inc=1, device_id={axis: peer}, device_id_type=MESH)
    pl.semaphore_wait(barrier, len(peers))


def send(src, dst, ssem, rsem, axis, peer):
    return pltpu.make_async_remote_copy(
        src_ref=src,
        dst_ref=dst,
        send_sem=ssem,
        recv_sem=rsem,
        device_id={axis: peer},
        device_id_type=MESH,
    )


def group_prefix(value, lane):
    for shift in (1, 2, 4):
        value = value + jnp.where(lane >= shift, pltpu.roll(value, shift, 1), 0)
    return value


def place_table(owners, picks, index, lane):
    shape = index.shape
    hits = [jnp.broadcast_to(owners[j : j + 1], shape) == index for j in range(3)]
    named = jnp.zeros(shape, jnp.int32)
    chosen = jnp.zeros(shape, jnp.int32)
    entry = lane * 3
    for j in range(3):
        named = named + jnp.where(hits[j], 1, 0)
        chosen = chosen + jnp.where(hits[j], jnp.broadcast_to(picks[j : j + 1], shape), 0)
        entry = entry + jnp.where(hits[j], j, 0)
    place = group_prefix(named, lane) - named
    mine = [(named == 1) & (place == k) for k in range(2)]
    table = [group_prefix(jnp.where(m, chosen + 1, 0), lane) - 1 for m in mine]
    return hits, entry, place, mine, table


def index_tables(owner_ref, block_ref, out, z, y):
    low = z < NZ // 2
    owners = jnp.where(low, owner_ref[:, :128], owner_ref[:, 128:])
    picks = jnp.where(low, block_ref[:, :128], block_ref[:, 128:])
    shape = (OWNERS, 128)
    index = lax.broadcasted_iota(jnp.int32, shape, 0)
    lane = lax.broadcasted_iota(jnp.int32, shape, 1) & 7
    hits, entry, place, mine, table = place_table(owners, picks, index, lane)
    for k in range(2):
        out[k * OWNERS : (k + 1) * OWNERS, :] = jnp.maximum(table[k], 0)
        out[RAW + k * OWNERS : RAW + (k + 1) * OWNERS, :] = table[k]
        out[ENTRY + k * OWNERS : ENTRY + (k + 1) * OWNERS, :] = group_prefix(
            jnp.where(mine[k], entry, 0), lane
        )
    for j in range(3):
        owner = owners[j : j + 1]
        at = jnp.minimum(jnp.sum(jnp.where(hits[j], place, 0), axis=0, keepdims=True), 1)
        zo = owner >> 2
        rel = ((owner & 3) - y + NY) & 3
        first = jnp.where(rel == 1, FROM_UP, jnp.where(rel == 2, FROM_FAR, FROM_DOWN))
        column = jnp.where(
            zo == lax.rem(z + NZ // 2, NZ), OPPOSITE + at, zo * RUN + picks[j : j + 1]
        )
        out[LISTS + j : LISTS + j + 1, :] = jnp.where(rel == 0, column, first + zo * 2 + at)
    owners = jnp.where(low, owner_ref[:, 128:], owner_ref[:, :128])
    picks = jnp.where(low, block_ref[:, 128:], block_ref[:, :128])
    table = place_table(owners, picks, index, lane)[4]
    for k in range(2):
        out[FAR + k * OWNERS : FAR + (k + 1) * OWNERS, :] = jnp.maximum(table[k], 0)
        out[FAR_RAW + k * OWNERS : FAR_RAW + (k + 1) * OWNERS, :] = table[k]


def whole_kernel(
    owner_hbm, block_hbm, k_ref, v_ref, q_hbm, do_hbm, wq_hbm, wk_hbm, wv_hbm, out,
    owner_ref, block_ref, tables, idx, tab, stage, ysend, osend, q_ref, do_ref, dq_ref, kl, vl, wacc, gacc, rp,
    halo, glob, wq, wkv, dkv, rsend, ybuf, obuf, hbuf, gbuf, pickers, acc, zup, zdown,
    total_ref, term, pair, xout, xin,
    ts, ws, zs, zr, ys, yr, hs, hr, gs, gr,
    zs2, zr2, ys2, yr2, hs2, hr2, gs2, gr2, ps, pr, xs, xr,
    os1, or1, os2, or2, og
):
    s, z, y = seq_place()
    zu, zd, yp, ym, y2 = neighbours(z, y)
    ypeers = (yp, ym, y2)
    h = lax.axis_index("head")
    x = lax.div(h, 2)
    c = lax.rem(h, 2)
    partner = x * 2 + 1 - c
    xpeers = (lax.rem(x + 1, NX) * 2 + c, lax.rem(x + NX - 1, NX) * 2 + c)
    plane = lax.rem(z, NZ // 2) * (NY * RUN) + RUN - 1
    own = (k_ref, v_ref)
    opp = lax.rem(z + NZ // 2, NZ)
    near = [lax.rem(z + n, NZ) for n in NEAR]

    loads = (
        pltpu.make_async_copy(q_hbm, q_ref, ws.at[0]),
        pltpu.make_async_copy(do_hbm, do_ref, ws.at[1]),
        pltpu.make_async_copy(wq_hbm, wq, ws.at[2]),
        pltpu.make_async_copy(wk_hbm, wkv.at[:, pl.ds(0, HD)], ws.at[3]),
        pltpu.make_async_copy(wv_hbm, wkv.at[:, pl.ds(HD, HD)], ws.at[4]),
    )
    mine = rows_of(z * ROWS, ROWS)
    first = (
        pltpu.make_async_copy(owner_hbm, owner_ref, ws.at[5]),
        pltpu.make_async_copy(block_hbm, block_ref, ws.at[6]),
        pltpu.make_async_copy(k_ref, tab.at[0, mine], ws.at[7]),
        pltpu.make_async_copy(v_ref, tab.at[1, mine], ws.at[8]),
    )
    for load in first:
        load.start()
    greet(
        [("seq", n) for n in (zu, zd, yp, ym, y2)]
        + [("seq", opp * NY + n) for n in range(NY)]
        + [("head", n) for n in (partner,) + xpeers]
    )

    def ring(up, t, kv, half):
        chunk = lax.rem(z + (NZ - t if up else t), NZ)
        where = tab.at[kv, rows_of(chunk * ROWS + half * HALF, HALF)]
        i = 0 if up else 1
        n = kv * 2 + half
        return send(
            own[kv].at[pl.ds(half * HALF, HALF)] if t == 0 else where, where,
            zs.at[i, t, n], zr.at[i, t, n], "seq", zu if up else zd,
        )

    def landed(up, t, kv, half):
        chunk = lax.rem(z + (NZ - 1 - t if up else 1 + t), NZ)
        where = tab.at[kv, rows_of(chunk * ROWS + half * HALF, HALF)]
        i = 0 if up else 1
        n = kv * 2 + half
        return send(where, where, zs.at[i, t, n], zr.at[i, t, n], "seq", zu if up else zd)

    def slot_copy(p, chunk, kv):
        first = (FROM_DOWN, FROM_UP, FROM_FAR)[p]
        at = rows_of((first + chunk * 2) * BLOCK, 2 * BLOCK)
        return send(
            ysend.at[p, chunk, kv], tab.at[kv, at, :], ys.at[p, chunk, kv], yr.at[p, chunk, kv],
            "seq", ypeers[p],
        )

    def opposite_copy(rel, chunk, kv):
        first = (OPPOSITE, FROM_DOWN + chunk * 2, FROM_FAR + chunk * 2, FROM_UP + chunk * 2)[rel]
        at = rows_of(first * BLOCK, 2 * BLOCK)
        return send(
            osend.at[rel, kv], tab.at[kv, at, :], os1.at[rel, kv], or1.at[rel, kv],
            "seq", opp * NY + lax.rem(y + rel, NY),
        )

    def opposite_global(n, kv):
        return send(
            tab.at[kv, pl.ds(0, 2 * BLOCK), :],
            tab.at[kv, pl.ds((EXTRA + 2) * BLOCK, 2 * BLOCK), :],
            og.at[n, kv], gr.at[kv], "seq", opp * NY + n,
        )

    def global_copy(p, kv):
        return send(
            tab.at[kv, pl.ds(0, 2 * BLOCK), :],
            tab.at[kv, pl.ds((EXTRA + 2) * BLOCK, 2 * BLOCK), :],
            gs.at[p, kv], gr.at[kv], "seq", ypeers[p],
        )

    def halo_copy(p, kv):
        if p == 0:
            row = lax.rem(z + NZ - lax.div(y, 3), NZ) * ROWS + (RUN - 1) * BLOCK
        else:
            row = lax.rem(z + lax.div(3 - y, 3), NZ) * ROWS
        at = pl.ds((EXTRA + p) * BLOCK, BLOCK)
        return send(
            tab.at[kv, rows_of(row, BLOCK), :], tab.at[kv, at, :], hs.at[p, kv], hr.at[p, kv],
            "seq", ypeers[p],
        )

    def spread(chunk, kv):
        stage[kv] = tab[kv, rows_of(chunk * ROWS, ROWS), :].reshape(RUN, BLOCK, HD)
        for p, rel in ((2, 2), (0, 1), (1, 3)):
            for k in range(2):
                pick = idx[k * OWNERS + chunk * NY + y, plane + lax.rem(y + rel, NY) * RUN]
                ysend[p, chunk, kv, k * BLOCK : (k + 1) * BLOCK, :] = stage[kv, pick]
        for p in (2, 0, 1):
            slot_copy(p, chunk, kv).start()

        @pl.when(jnp.logical_and(chunk == 0, y == 0))
        def _():
            for p in range(3):
                global_copy(p, kv).start()

    for kv in range(2):
        for half in range(2):
            ring(True, 0, kv, half).start()
            ring(False, 0, kv, half).start()
    first[0].wait()
    first[1].wait()
    index_tables(owner_ref, block_ref, tables, z, y)
    to_scalar = pltpu.make_async_copy(tables, idx, ts)
    to_scalar.start()
    first[2].wait()
    first[3].wait()
    to_scalar.wait()
    for kv in range(2):
        spread(z, kv)
        for rel in range(NY):
            for k in range(2):
                pick = idx[FAR + k * OWNERS + z * NY + y, plane + lax.rem(y + rel, NY) * RUN]
                osend[rel, kv, k * BLOCK : (k + 1) * BLOCK, :] = stage[kv, pick]
    for load in loads:
        load.start()
    for t in range(3):
        for kv in range(2):
            for half in range(2):
                for up in (True, False):
                    landed(up, t, kv, half).wait_recv()
                    if t < 2:
                        ring(up, t + 1, kv, half).start()
            for up in (True, False):
                spread(lax.rem(z + (NZ - 1 - t if up else 1 + t), NZ), kv)
            if t == 0:
                for p in range(2):
                    halo_copy(p, kv).start()
            if t == 1:
                for rel in (2, 1, 3, 0):
                    opposite_copy(rel, z, kv).start()

                @pl.when(s == 0)
                def _():
                    for n in range(NY):
                        opposite_global(n, kv).start()

    loads[0].wait()
    loads[1].wait()
    wacc[...] = jnp.zeros_like(wacc)
    gacc[...] = jnp.zeros_like(gacc)
    for kv in range(2):
        for p in range(3):
            for chunk in near:
                slot_copy(p, chunk, kv).wait_recv()
        for p in range(2):
            halo_copy(p, kv).wait_recv()
        for rel in range(NY):
            opposite_copy(rel, opp, kv).wait_recv()

        @pl.when(jnp.logical_and(y == 0, z != NZ // 2))
        def _():
            tab[kv, (EXTRA + 2) * BLOCK : (EXTRA + 4) * BLOCK, :] = tab[kv, 0 : 2 * BLOCK, :]

        @pl.when(jnp.logical_or(y != 0, z == NZ // 2))
        def _():
            global_copy(0, kv).wait_recv()

    def attend(step, carry):
        grads = []
        for n in range(PER):
            b = step * PER + n
            index = [
                jnp.where(b == 0, EXTRA, z * RUN + b - 1),
                z * RUN + b,
                jnp.where(b == RUN - 1, EXTRA + 1, z * RUN + b + 1),
                EXTRA + 2,
                EXTRA + 3,
            ] + [idx[LISTS + j, plane - (RUN - 1) + y * RUN + b] for j in range(3)]
            for j in range(8):
                at = index[j]
                kl[n, j * BLOCK : (j + 1) * BLOCK, :] = tab_blocks[0, at]
                vl[n, j * BLOCK : (j + 1) * BLOCK, :] = tab_blocks[1, at]
        for n in range(PER):
            b = step * PER + n
            mine = rows_of(b * BLOCK, BLOCK)
            q4 = jnp.concatenate([q_ref[mine, g * HD : (g + 1) * HD] for g in range(GROUP)], axis=0)
            d4 = jnp.concatenate([do_ref[mine, g * HD : (g + 1) * HD] for g in range(GROUP)], axis=0)
            keys = kl[n]
            vals = vl[n]
            scores = dot(keys, q4, NT)
            no_left = jnp.logical_and(s == 0, b == 0)
            no_right = jnp.logical_and(s == NZ * NY - 1, b == RUN - 1)
            scores = jnp.concatenate(
                [
                    jnp.where(no_left, -1e30, scores[:BLOCK]),
                    scores[BLOCK : 2 * BLOCK],
                    jnp.where(no_right, -1e30, scores[2 * BLOCK : 3 * BLOCK]),
                    scores[3 * BLOCK :],
                ],
                axis=0,
            )
            row_max = jnp.max(scores, axis=0, keepdims=True)
            powers = jnp.exp((scores - row_max) * SCALE)
            weights = powers * (1.0 / jnp.sum(powers, axis=0, keepdims=True))
            weights_half = weights.astype(jnp.bfloat16)
            dprob = dot(vals, d4, NT)
            delta = jnp.sum(weights_half.astype(jnp.float32) * dprob, axis=0, keepdims=True)
            dscore_half = (weights * (dprob - delta)).astype(jnp.bfloat16)
            dq = (dot(dscore_half, keys, TN) * SCALE).astype(jnp.bfloat16)
            for g in range(GROUP):
                dq_ref[mine, g * HD : (g + 1) * HD] = dq[g * BLOCK : (g + 1) * BLOCK]
            grads.append((dot(dscore_half, q4, NN) * SCALE, dot(weights_half, d4, NN)))
        for n in range(PER):
            b = step * PER + n
            for kv in range(2):
                grad = grads[n][kv]
                wacc[kv, rows_of(b * BLOCK, 3 * BLOCK), :] += grad[: 3 * BLOCK]
                gacc[kv] += grad[3 * BLOCK : 5 * BLOCK]
                for j in range(3):
                    rp[kv, b * 3 + j] = grad[(5 + j) * BLOCK : (6 + j) * BLOCK].astype(jnp.bfloat16)
        return carry

    tab_blocks = tab.reshape(2, TABLE, BLOCK, HD)
    lax.fori_loop(0, RUN // PER, attend, 0)
    for kv in range(2):
        halo[kv, :BLOCK, :] = wacc[kv, :BLOCK, :].astype(jnp.bfloat16)
        halo[kv, BLOCK:, :] = wacc[kv, BLOCK + ROWS :, :].astype(jnp.bfloat16)
        glob[kv] = gacc[kv].astype(jnp.bfloat16)

    def back_copy(p, chunk, kv):
        return send(
            rsend.at[p, chunk, kv], ybuf.at[p, chunk, kv], ys2.at[p, chunk, kv],
            yr2.at[p, chunk, kv], "seq", ypeers[p],
        )

    def halo_back(p, kv):
        half = pl.ds(BLOCK if p == 0 else 0, BLOCK)
        return send(
            halo.at[kv, half, :], hbuf.at[p, kv], hs2.at[p, kv], hr2.at[p, kv],
            "seq", ypeers[p],
        )

    def global_back(slot, kv):
        return send(
            glob.at[kv], gbuf.at[slot, kv], gs2.at[kv], gr2.at[slot, kv], "seq",
            z * NY if slot < 3 else 0,
        )

    def opposite_back(rel, kv):
        return send(
            osend.at[rel, kv], obuf.at[rel, kv], os2.at[rel, kv], or2.at[rel, kv],
            "seq", opp * NY + lax.rem(y + rel, NY),
        )

    def offer_opposite(kv):
        for rel in range(NY):
            opposite_copy(rel, z, kv).wait_send()
        for rel in range(NY):
            for k in range(2):
                osend[rel, kv, k * BLOCK : (k + 1) * BLOCK, :] = rp[kv, entry_of(k, opp, rel)]
        for rel in (2, 1, 3, 0):
            opposite_back(rel, kv).start()

    def select(slot, n, first, second):
        lane = lax.broadcasted_iota(jnp.int32, (1, HD), 1)
        row = lax.broadcasted_iota(jnp.int32, (ROWS, HD), 0)
        target = jnp.where(lane < BLOCK, first, second) * BLOCK + (lane & (BLOCK - 1))
        pickers[slot, :, n * HD : (n + 1) * HD] = jnp.where(
            row == target, 1.0, 0.0
        ).astype(jnp.bfloat16)

    events = []
    for m in (3, 2, 1):
        events += [(m, 1, 0), (-m, 0, 1), (m, 0, 0), (-m, 1, 1)]
    events += [(0, 0, None), (0, 1, None)]
    low_chunk = lax.rem(z + NZ - lax.div(y, 3), NZ)
    high_chunk = lax.rem(z + lax.div(3 - y, 3), NZ)

    def entry_of(k, chunk, rel):
        return idx[ENTRY + k * OWNERS + chunk * NY + lax.rem(y + rel, NY), plane + y * RUN]

    def offer(event):
        off, kv, _ = event
        chunk = lax.rem(z + off + NZ, NZ)
        for p, rel in ((2, 2), (0, 1), (1, 3)):
            for k in range(2):
                rsend[p, chunk, kv, k * BLOCK : (k + 1) * BLOCK, :] = rp[kv, entry_of(k, chunk, rel)]
        for p in (2, 0, 1):
            back_copy(p, chunk, kv).start()

    done = []

    def collect(event):
        off, kv, _ = event
        chunk = lax.rem(z + off + NZ, NZ)
        for p in range(3):
            back_copy(p, chunk, kv).wait_recv()
        slot = 1 if off < 0 else 0
        if (off, 1 - kv) not in done:
            for n, rel in enumerate((0, 3, 1, 2)):
                first, second = [
                    idx[RAW + k * OWNERS + chunk * NY + y, plane + lax.rem(y + rel, NY) * RUN]
                    for k in range(2)
                ]
                select(slot, n, first, second)
            if off == 0:
                for rel in range(NY):
                    lane = plane + lax.rem(y + NY - rel, NY) * RUN
                    first, second = [
                        idx[FAR_RAW + k * OWNERS + z * NY + y, lane] for k in range(2)
                    ]
                    select(2, rel, first, second)
        done.append((off, kv))
        data = [rp[kv, entry_of(k, chunk, 0)] for k in range(2)]
        data += [ybuf[p, chunk, kv] for p in range(3)]
        sums = dot(pickers[slot], jnp.concatenate(data, axis=0), NN)
        if off == 0:
            for rel in range(NY):
                opposite_back(rel, kv).wait_recv()
            data = [obuf[rel, kv] for rel in range(NY)]
            sums = sums + dot(pickers[2], jnp.concatenate(data, axis=0), NN)
        acc[kv] = sums

        @pl.when(chunk == low_chunk)
        def _():
            halo_back(1, kv).wait_recv()
            acc[kv, (RUN - 1) * BLOCK :, :] += hbuf[1, kv].astype(jnp.float32)

        @pl.when(chunk == high_chunk)
        def _():
            halo_back(0, kv).wait_recv()
            acc[kv, :BLOCK, :] += hbuf[0, kv].astype(jnp.float32)

        @pl.when(jnp.logical_and(chunk == 0, y == 0))
        def _():
            total = glob[kv].astype(jnp.float32)
            for m in range(3):
                global_back(m, kv).wait_recv()
                total = total + gbuf[m, kv].astype(jnp.float32)
            acc[kv, 0 : 2 * BLOCK, :] += total

        if off == 0:
            @pl.when(s == 0)
            def _():
                total = jnp.zeros((2 * BLOCK, HD), jnp.float32)
                for m in range(3, 7):
                    global_back(m, kv).wait_recv()
                    total = total + gbuf[m, kv].astype(jnp.float32)
                acc[kv, 0 : 2 * BLOCK, :] += total

    bufs = (zup, zdown)
    zpeer = (zu, zd)

    def zring(i, t, kv, n):
        at = pl.ds(n * HALF, HALF) if t < 2 else token_rows(n)
        return send(
            bufs[i].at[0, t, kv, at], bufs[i].at[1, t, kv, at], zs2.at[i, t, kv, n],
            zr2.at[i, t, kv, n], "seq", zpeer[i],
        )

    def zpush(event):
        off, kv, i = event
        t = 3 - abs(off)
        for half in range(2):
            at = pl.ds(half * HALF, HALF)
            total = acc[kv, at, :]
            if t >= 1:
                zring(i, t - 1, kv, half).wait_recv()
                total = total + bufs[i][1, t - 1, kv, at, :].astype(jnp.float32)
            bufs[i][0, t, kv, at, :] = total.astype(jnp.bfloat16)
            if t < 2:
                zring(i, t, kv, half).start()
        if t == 2:
            for d in (2, 1, 3, 0):
                zring(i, t, kv, d).start()

    def token_rows(d):
        return rows_of(lax.rem(x + d, NX) * 2 * BLOCK, 2 * BLOCK)

    def query_part(n):
        d = (2, 1, 3, 0)[n // 2]
        a = dq_ref[token_rows(d), :]

        def tile(m, carry):
            w = pl.ds(pl.multiple_of(m * TILE, TILE), TILE)
            total_ref[d, :, w] = dot(a, wq[w, :], NT)
            return carry

        half = D // TILE // 2
        lax.fori_loop(n % 2 * half, n % 2 * half + half, tile, 0)

    ahead = 6
    for n, event in enumerate(events[:ahead]):
        if n < 2:
            for m in range(NY):
                if m > 0:
                    @pl.when(jnp.logical_and(y == m, z != NZ // 2))
                    def _():
                        global_back(m - 1, n).start()

                @pl.when(jnp.logical_and(y == m, z == NZ // 2))
                def _():
                    global_back(3 + m, n).start()
        offer(event)
    for p in range(2):
        for kv in range(2):
            halo_back(p, kv).start()
    for load in loads[2:]:
        load.wait()
    query_part(0)
    query_part(1)

    parts = 2
    for n, event in enumerate(events[:12]):
        collect(event)
        zpush(event)
        if n + ahead < 14:
            offer(events[n + ahead])
        if n in (5, 6):
            offer_opposite(n - 5)
        if n % 2 == 1 and parts < 8:
            query_part(parts)
            parts += 1
    for kv in range(2):
        collect(events[12 + kv])

    def settle(d):
        at = token_rows(d)
        shifted = rows_of(lax.rem(x + d, NX) * 2 * BLOCK + BLOCK, 2 * BLOCK)
        for kv in range(2):
            total = acc[kv, at, :] + wacc[kv, shifted, :]
            for i in range(2):
                zring(i, 2, kv, d).wait_recv()
                total = total + bufs[i][1, 2, kv, at, :].astype(jnp.float32)
            dkv[at, kv * HD : (kv + 1) * HD] = total.astype(jnp.bfloat16)

    def cols(quarter):
        return pl.ds(quarter * QUARTER, QUARTER)

    def pair_copy(d, quarter):
        return send(
            term.at[d, rows_of((1 - c) * BLOCK, BLOCK), cols(quarter)],
            pair.at[d, :, cols(quarter)], ps.at[d, quarter], pr.at[d, quarter],
            "head", partner,
        )

    def xring(i, t, quarter):
        return send(
            xout.at[i, t, :, cols(quarter)], xin.at[i, t, :, cols(quarter)],
            xs.at[i, t, quarter], xr.at[i, t, quarter], "head", xpeers[i],
        )

    def compute(d):
        settle(d)
        a = dkv[token_rows(d), :]
        for quarter in range(4):
            def tile(n, carry):
                w = pl.ds(pl.multiple_of(quarter * QUARTER + n * TILE, TILE), TILE)
                total = total_ref[d, :, w] + dot(a, wkv[w, :], NT)
                term[d, :, w] = total.astype(jnp.bfloat16)
                return carry

            lax.fori_loop(0, QUARTER // TILE, tile, 0)
            pair_copy(d, quarter).start()

    def both(d, quarter):
        pair_copy(d, quarter).wait_recv()
        mine = term[d, rows_of(c * BLOCK, BLOCK), cols(quarter)].astype(jnp.float32)
        return mine + pair[d, :, cols(quarter)].astype(jnp.float32)

    def arrived(i, t, quarter):
        xring(i, t, quarter).wait_recv()
        return xin[i, t, :, cols(quarter)].astype(jnp.float32)

    def xpush(i, t, quarter, total):
        xout[i, t, :, cols(quarter)] = total.astype(jnp.bfloat16)
        xring(i, t, quarter).start()

    compute(2)
    compute(1)
    for n in range(2):
        xpush(0, 0, n, both(2, n))
        xpush(1, 0, 2 + n, both(2, 2 + n))
    compute(3)
    for n in range(2):
        xpush(0, 1, 2 + n, both(1, 2 + n))
        xpush(1, 1, n, both(3, n))
    compute(0)
    for n in range(2):
        xpush(0, 1, n, both(1, n) + arrived(0, 0, n))
        xpush(1, 1, 2 + n, both(3, 2 + n) + arrived(1, 0, 2 + n))
    for quarter in (2, 3, 0, 1):
        total = both(0, quarter) + arrived(0, 1, quarter) + arrived(1, 1, quarter)
        out[:, cols(quarter)] = total.astype(jnp.bfloat16)

    for i in range(2):
        for t in range(3):
            for kv in range(2):
                for half in range(2):
                    ring(i == 0, t, kv, half).wait_send()
                for n in range(2 if t < 2 else 4):
                    zring(i, t, kv, n).wait_send()
    for p in range(3):
        for chunk in near:
            for kv in range(2):
                slot_copy(p, chunk, kv).wait_send()
                back_copy(p, chunk, kv).wait_send()
    for rel in range(NY):
        for kv in range(2):
            opposite_back(rel, kv).wait_send()

    @pl.when(s == 0)
    def _():
        for n in range(NY):
            for kv in range(2):
                opposite_global(n, kv).wait_send()

    for p in range(2):
        for kv in range(2):
            halo_copy(p, kv).wait_send()
            halo_back(p, kv).wait_send()

    @pl.when(jnp.logical_and(y == 0, z != NZ // 2))
    def _():
        for p in range(3):
            for kv in range(2):
                global_copy(p, kv).wait_send()

    @pl.when(jnp.logical_or(y != 0, z == NZ // 2))
    def _():
        for kv in range(2):
            global_back(0, kv).wait_send()

    for d in range(4):
        for quarter in range(4):
            pair_copy(d, quarter).wait_send()
    for i in range(2):
        for quarter in range(4):
            if quarter // 2 == i:
                xring(i, 0, quarter).wait_send()
            xring(i, 1, quarter).wait_send()


def whole(owners, blocks, keys, values, query, grad_out, wq, wk, wv):
    anywhere = pl.BlockSpec(memory_space=pltpu.HBM)
    half = jnp.bfloat16
    full = jnp.float32
    slots = (3, NZ, 2, 2 * BLOCK, HD)
    return pl.pallas_call(
        whole_kernel,
        out_shape=sds((BLOCK, D)),
        in_specs=[anywhere] * 9,
        out_specs=vmem(),
        scratch_shapes=[
            VM((3, OWNERS * RUN), jnp.int32),
            VM((3, OWNERS * RUN), jnp.int32),
            VM((INDEX_ROWS, 128), jnp.int32),
            pltpu.SMEM((INDEX_ROWS, 128), jnp.int32),
            VM((2, TABLE * BLOCK, HD), half),
            VM((2, RUN, BLOCK, HD), half),
            VM(slots, half),
            VM((NY, 2, 2 * BLOCK, HD), half),
            VM((ROWS, GROUP * HD), half),
            VM((ROWS, GROUP * HD), half),
            VM((ROWS, GROUP * HD), half),
            VM((PER, ROWS, HD), half),
            VM((PER, ROWS, HD), half),
            VM((2, ROWS + 2 * BLOCK, HD), full),
            VM((2, 2 * BLOCK, HD), full),
            VM((2, RUN * 3, BLOCK, HD), half),
            VM((2, 2 * BLOCK, HD), half),
            VM((2, 2 * BLOCK, HD), half),
            VM((D, GROUP * HD), half),
            VM((D, 2 * HD), half),
            VM((ROWS, 2 * HD), half),
            VM(slots, half),
            VM(slots, half),
            VM((NY, 2, 2 * BLOCK, HD), half),
            VM((2, 2, BLOCK, HD), half),
            VM((7, 2, 2 * BLOCK, HD), half),
            VM((3, ROWS, ROWS), half),
            VM((2, ROWS, HD), full),
            VM((2, 4, 2, ROWS, HD), half),
            VM((2, 4, 2, ROWS, HD), half),
            VM((4, 2 * BLOCK, D), full),
            VM((4, 2 * BLOCK, D), half),
            VM((4, BLOCK, D), half),
            VM((2, 2, BLOCK, D), half),
            VM((2, 2, BLOCK, D), half),
            DMA,
            DMA((9,)),
            DMA((2, 4, 4)),
            DMA((2, 4, 4)),
            DMA((3, NZ, 2)),
            DMA((3, NZ, 2)),
            DMA((2, 2)),
            DMA((2, 2)),
            DMA((3, 2)),
            DMA((2,)),
            DMA((2, 4, 2, 4)),
            DMA((2, 4, 2, 4)),
            DMA((3, NZ, 2)),
            DMA((3, NZ, 2)),
            DMA((2, 2)),
            DMA((2, 2)),
            DMA((2,)),
            DMA((7, 2)),
            DMA((4, 4)),
            DMA((4, 4)),
            DMA((2, 2, 4)),
            DMA((2, 2, 4)),
            DMA((NY, 2)),
            DMA((NY, 2)),
            DMA((NY, 2)),
            DMA((NY, 2)),
            DMA((NY, 2)),
        ],
        compiler_params=pltpu.CompilerParams(
            collective_id=0, has_side_effects=True, vmem_limit_bytes=60 * 2**20
        ),
        name="whole",
    )(owners, blocks, keys, values, query, grad_out, wq, wk, wv)


def on_device(query, keys, values, grad_out, w_query, w_key, w_value, rand_owner, rand_block):
    return whole(
        rand_owner.T, rand_block.T, keys, values, query, grad_out, w_query, w_key, w_value
    )


def solution(mesh):
    return jax.shard_map(
        on_device,
        mesh=mesh,
        in_specs=(
            P("seq", "head"),
            P("seq", "head"),
            P("seq", "head"),
            P("seq", "head"),
            P(None, "head"),
            P(None, "head"),
            P(None, "head"),
            P(),
            P(),
        ),
        out_specs=P(("seq", "head"), None),
        check_vma=False,
    )
```

```python
import functools

import jax
import jax.numpy as jnp
from jax import lax
from jax.experimental import pallas as pl
from jax.experimental.pallas import tpu as pltpu
from jax.sharding import PartitionSpec as P

BLOCK = 64
HD = 128
NZ = 8
NY = 4
NX = 4
RUN = 8
ROWS = RUN * BLOCK
HALF = ROWS // 2
GROUP = 4
D = 4096
FROM_UP = NZ * RUN
FROM_DOWN = FROM_UP + 2 * NZ
FROM_FAR = FROM_DOWN + 2 * NZ
EXTRA = FROM_FAR + 2 * NZ
TABLE = EXTRA + 4
OWNERS = NZ * NY
RAW = 2 * OWNERS
ENTRY = 4 * OWNERS
LISTS = 6 * OWNERS
QUARTER = D // 4
TILE = 512
PER = 2
MESH = pl.DeviceIdType.MESH
SCALE = HD ** (-0.5)
VM = pltpu.VMEM
DMA = pltpu.SemaphoreType.DMA
NT = (((1,), (1,)), ((), ()))
NN = (((1,), (0,)), ((), ()))
TN = (((0,), (0,)), ((), ()))


def vmem():
    return pl.BlockSpec(memory_space=pltpu.VMEM)


def sds(shape, dtype=jnp.bfloat16):
    return jax.ShapeDtypeStruct(shape, dtype)


def dot(a, b, dims):
    return lax.dot_general(a, b, dims, preferred_element_type=jnp.float32)


def seq_place():
    s = lax.axis_index("seq")
    return s, lax.div(s, NY), lax.rem(s, NY)


def rows_of(start, size):
    return pl.ds(pl.multiple_of(start, BLOCK), size)


def neighbours(z, y):
    return (
        lax.rem(z + 1, NZ) * NY + y,
        lax.rem(z + NZ - 1, NZ) * NY + y,
        z * NY + lax.rem(y + 1, NY),
        z * NY + lax.rem(y + 3, NY),
        z * NY + lax.rem(y + 2, NY),
    )


def greet(peers):
    barrier = pltpu.get_barrier_semaphore()
    for axis, peer in peers:
        pl.semaphore_signal(barrier, inc=1, device_id={axis: peer}, device_id_type=MESH)
    pl.semaphore_wait(barrier, len(peers))


def send(src, dst, ssem, rsem, axis, peer):
    return pltpu.make_async_remote_copy(
        src_ref=src,
        dst_ref=dst,
        send_sem=ssem,
        recv_sem=rsem,
        device_id={axis: peer},
        device_id_type=MESH,
    )


def group_prefix(value, lane):
    for shift in (1, 2, 4):
        value = value + jnp.where(lane >= shift, pltpu.roll(value, shift, 1), 0)
    return value


def index_tables(owner_ref, block_ref, out, z, y):
    low = z < NZ // 2
    owners = jnp.where(low, owner_ref[:, :128], owner_ref[:, 128:])
    picks = jnp.where(low, block_ref[:, :128], block_ref[:, 128:])
    shape = (OWNERS, 128)
    index = lax.broadcasted_iota(jnp.int32, shape, 0)
    lane = lax.broadcasted_iota(jnp.int32, shape, 1) & 7
    hits = [jnp.broadcast_to(owners[j : j + 1], shape) == index for j in range(3)]
    named = jnp.zeros(shape, jnp.int32)
    chosen = jnp.zeros(shape, jnp.int32)
    entry = lane * 3
    for j in range(3):
        named = named + jnp.where(hits[j], 1, 0)
        chosen = chosen + jnp.where(hits[j], jnp.broadcast_to(picks[j : j + 1], shape), 0)
        entry = entry + jnp.where(hits[j], j, 0)
    place = group_prefix(named, lane) - named
    for k in range(2):
        mine = (named == 1) & (place == k)
        pick = group_prefix(jnp.where(mine, chosen + 1, 0), lane) - 1
        out[k * OWNERS : (k + 1) * OWNERS, :] = jnp.maximum(pick, 0)
        out[RAW + k * OWNERS : RAW + (k + 1) * OWNERS, :] = pick
        out[ENTRY + k * OWNERS : ENTRY + (k + 1) * OWNERS, :] = group_prefix(
            jnp.where(mine, entry, 0), lane
        )
    for j in range(3):
        owner = owners[j : j + 1]
        at = jnp.minimum(jnp.sum(jnp.where(hits[j], place, 0), axis=0, keepdims=True), 1)
        zo = owner >> 2
        rel = ((owner & 3) - y + NY) & 3
        first = jnp.where(rel == 1, FROM_UP, jnp.where(rel == 2, FROM_FAR, FROM_DOWN))
        out[LISTS + j : LISTS + j + 1, :] = jnp.where(
            rel == 0, zo * RUN + picks[j : j + 1], first + zo * 2 + at
        )


def whole_kernel(
    owner_hbm, block_hbm, k_ref, v_ref, q_hbm, do_hbm, wq_hbm, wk_hbm, wv_hbm, out,
    owner_ref, block_ref, tables, idx, tab, stage, ysend, q_ref, do_ref, dq_ref, kl, vl, wacc, gacc, rp,
    halo, glob, wq, wkv, dkv, rsend, ybuf, hbuf, gbuf, pickers, acc, zup, zdown,
    total_ref, term, pair, xout, xin,
    ts, ws, zs, zr, ys, yr, hs, hr, gs, gr,
    zs2, zr2, ys2, yr2, hs2, hr2, gs2, gr2, ps, pr, xs, xr
):
    s, z, y = seq_place()
    zu, zd, yp, ym, y2 = neighbours(z, y)
    ypeers = (yp, ym, y2)
    h = lax.axis_index("head")
    x = lax.div(h, 2)
    c = lax.rem(h, 2)
    partner = x * 2 + 1 - c
    xpeers = (lax.rem(x + 1, NX) * 2 + c, lax.rem(x + NX - 1, NX) * 2 + c)
    plane = lax.rem(z, NZ // 2) * (NY * RUN) + RUN - 1
    own = (k_ref, v_ref)

    loads = (
        pltpu.make_async_copy(q_hbm, q_ref, ws.at[0]),
        pltpu.make_async_copy(do_hbm, do_ref, ws.at[1]),
        pltpu.make_async_copy(wq_hbm, wq, ws.at[2]),
        pltpu.make_async_copy(wk_hbm, wkv.at[:, pl.ds(0, HD)], ws.at[3]),
        pltpu.make_async_copy(wv_hbm, wkv.at[:, pl.ds(HD, HD)], ws.at[4]),
    )
    mine = rows_of(z * ROWS, ROWS)
    first = (
        pltpu.make_async_copy(owner_hbm, owner_ref, ws.at[5]),
        pltpu.make_async_copy(block_hbm, block_ref, ws.at[6]),
        pltpu.make_async_copy(k_ref, tab.at[0, mine], ws.at[7]),
        pltpu.make_async_copy(v_ref, tab.at[1, mine], ws.at[8]),
    )
    for load in first:
        load.start()
    greet(
        [("seq", n) for n in (zu, zd, yp, ym, y2)]
        + [("head", n) for n in (partner,) + xpeers]
    )

    def ring(up, t, kv, half):
        chunk = lax.rem(z + (NZ - t if up else t), NZ)
        where = tab.at[kv, rows_of(chunk * ROWS + half * HALF, HALF)]
        i = 0 if up else 1
        n = kv * 2 + half
        return send(
            own[kv].at[pl.ds(half * HALF, HALF)] if t == 0 else where, where,
            zs.at[i, t, n], zr.at[i, t, n], "seq", zu if up else zd,
        )

    def landed(up, t, kv, half):
        chunk = lax.rem(z + (NZ - 1 - t if up else 1 + t), NZ)
        where = tab.at[kv, rows_of(chunk * ROWS + half * HALF, HALF)]
        i = 0 if up else 1
        n = kv * 2 + half
        return send(where, where, zs.at[i, t, n], zr.at[i, t, n], "seq", zu if up else zd)

    def slot_copy(p, chunk, kv):
        first = (FROM_DOWN, FROM_UP, FROM_FAR)[p]
        at = rows_of((first + chunk * 2) * BLOCK, 2 * BLOCK)
        return send(
            ysend.at[p, chunk, kv], tab.at[kv, at, :], ys.at[p, chunk, kv], yr.at[p, chunk, kv],
            "seq", ypeers[p],
        )

    def global_copy(p, kv):
        return send(
            tab.at[kv, pl.ds(0, 2 * BLOCK), :],
            tab.at[kv, pl.ds((EXTRA + 2) * BLOCK, 2 * BLOCK), :],
            gs.at[p, kv], gr.at[kv], "seq", ypeers[p],
        )

    def halo_copy(p, kv):
        if p == 0:
            row = lax.rem(z + NZ - lax.div(y, 3), NZ) * ROWS + (RUN - 1) * BLOCK
        else:
            row = lax.rem(z + lax.div(3 - y, 3), NZ) * ROWS
        at = pl.ds((EXTRA + p) * BLOCK, BLOCK)
        return send(
            tab.at[kv, rows_of(row, BLOCK), :], tab.at[kv, at, :], hs.at[p, kv], hr.at[p, kv],
            "seq", ypeers[p],
        )

    def spread(chunk, kv):
        stage[kv] = tab[kv, rows_of(chunk * ROWS, ROWS), :].reshape(RUN, BLOCK, HD)
        for p, rel in ((2, 2), (0, 1), (1, 3)):
            for k in range(2):
                pick = idx[k * OWNERS + chunk * NY + y, plane + lax.rem(y + rel, NY) * RUN]
                ysend[p, chunk, kv, k * BLOCK : (k + 1) * BLOCK, :] = stage[kv, pick]
        for p in (0, 1, 2):
            slot_copy(p, chunk, kv).start()

        @pl.when(jnp.logical_and(chunk == 0, y == 0))
        def _():
            for p in range(3):
                global_copy(p, kv).start()

    for kv in range(2):
        for half in range(2):
            ring(True, 0, kv, half).start()
            ring(False, 0, kv, half).start()
    first[0].wait()
    first[1].wait()
    index_tables(owner_ref, block_ref, tables, z, y)
    to_scalar = pltpu.make_async_copy(tables, idx, ts)
    to_scalar.start()
    first[2].wait()
    first[3].wait()
    to_scalar.wait()
    for kv in range(2):
        spread(z, kv)
    for load in loads:
        load.start()
    for t in range(4):
        for kv in range(2):
            ups = (True, False) if t < 3 else ((True,) if kv == 0 else (False,))
            for half in range(2):
                for up in ups:
                    landed(up, t, kv, half).wait_recv()
                    if t < 2 or (t == 2 and kv == (0 if up else 1)):
                        ring(up, t + 1, kv, half).start()
            for up in ups:
                spread(lax.rem(z + (NZ - 1 - t if up else 1 + t), NZ), kv)
            if t == 0:
                for p in range(2):
                    halo_copy(p, kv).start()

    loads[0].wait()
    loads[1].wait()
    wacc[...] = jnp.zeros_like(wacc)
    gacc[...] = jnp.zeros_like(gacc)
    for kv in range(2):
        for p in range(3):
            for n in range(NZ):
                slot_copy(p, n, kv).wait_recv()
        for p in range(2):
            halo_copy(p, kv).wait_recv()

        @pl.when(y == 0)
        def _():
            tab[kv, (EXTRA + 2) * BLOCK : (EXTRA + 4) * BLOCK, :] = tab[kv, 0 : 2 * BLOCK, :]

        @pl.when(y != 0)
        def _():
            global_copy(0, kv).wait_recv()

    def attend(step, carry):
        grads = []
        for n in range(PER):
            b = step * PER + n
            index = [
                jnp.where(b == 0, EXTRA, z * RUN + b - 1),
                z * RUN + b,
                jnp.where(b == RUN - 1, EXTRA + 1, z * RUN + b + 1),
                EXTRA + 2,
                EXTRA + 3,
            ] + [idx[LISTS + j, plane - (RUN - 1) + y * RUN + b] for j in range(3)]
            for j in range(8):
                at = index[j]
                kl[n, j * BLOCK : (j + 1) * BLOCK, :] = tab_blocks[0, at]
                vl[n, j * BLOCK : (j + 1) * BLOCK, :] = tab_blocks[1, at]
        for n in range(PER):
            b = step * PER + n
            mine = rows_of(b * BLOCK, BLOCK)
            q4 = jnp.concatenate([q_ref[mine, g * HD : (g + 1) * HD] for g in range(GROUP)], axis=0)
            d4 = jnp.concatenate([do_ref[mine, g * HD : (g + 1) * HD] for g in range(GROUP)], axis=0)
            keys = kl[n]
            vals = vl[n]
            scores = dot(keys, q4, NT)
            no_left = jnp.logical_and(s == 0, b == 0)
            no_right = jnp.logical_and(s == NZ * NY - 1, b == RUN - 1)
            scores = jnp.concatenate(
                [
                    jnp.where(no_left, -1e30, scores[:BLOCK]),
                    scores[BLOCK : 2 * BLOCK],
                    jnp.where(no_right, -1e30, scores[2 * BLOCK : 3 * BLOCK]),
                    scores[3 * BLOCK :],
                ],
                axis=0,
            )
            row_max = jnp.max(scores, axis=0, keepdims=True)
            powers = jnp.exp((scores - row_max) * SCALE)
            weights = powers * (1.0 / jnp.sum(powers, axis=0, keepdims=True))
            weights_half = weights.astype(jnp.bfloat16)
            dprob = dot(vals, d4, NT)
            delta = jnp.sum(weights_half.astype(jnp.float32) * dprob, axis=0, keepdims=True)
            dscore_half = (weights * (dprob - delta)).astype(jnp.bfloat16)
            dq = (dot(keys, dscore_half, TN) * SCALE).T.astype(jnp.bfloat16)
            for g in range(GROUP):
                dq_ref[mine, g * HD : (g + 1) * HD] = dq[g * BLOCK : (g + 1) * BLOCK]
            grads.append((dot(dscore_half, q4, NN) * SCALE, dot(weights_half, d4, NN)))
        for n in range(PER):
            b = step * PER + n
            for kv in range(2):
                grad = grads[n][kv]
                wacc[kv, rows_of(b * BLOCK, 3 * BLOCK), :] += grad[: 3 * BLOCK]
                gacc[kv] += grad[3 * BLOCK : 5 * BLOCK]
                for j in range(3):
                    rp[kv, b * 3 + j] = grad[(5 + j) * BLOCK : (6 + j) * BLOCK].astype(jnp.bfloat16)
        return carry

    tab_blocks = tab.reshape(2, TABLE, BLOCK, HD)
    lax.fori_loop(0, RUN // PER, attend, 0)
    for kv in range(2):
        halo[kv, :BLOCK, :] = wacc[kv, :BLOCK, :].astype(jnp.bfloat16)
        halo[kv, BLOCK:, :] = wacc[kv, BLOCK + ROWS :, :].astype(jnp.bfloat16)
        glob[kv] = gacc[kv].astype(jnp.bfloat16)

    def back_copy(p, chunk, kv):
        return send(
            rsend.at[p, chunk, kv], ybuf.at[p, chunk, kv], ys2.at[p, chunk, kv],
            yr2.at[p, chunk, kv], "seq", ypeers[p],
        )

    def halo_back(p, kv):
        half = pl.ds(BLOCK if p == 0 else 0, BLOCK)
        return send(
            halo.at[kv, half, :], hbuf.at[p, kv], hs2.at[p, kv], hr2.at[p, kv],
            "seq", ypeers[p],
        )

    def global_back(slot, kv):
        return send(glob.at[kv], gbuf.at[slot, kv], gs2.at[kv], gr2.at[slot, kv], "seq", z * NY)

    events = [(4, 0, 0), (4, 1, 1)]
    for m in (3, 2, 1):
        events += [(m, 1, 0), (-m, 0, 1), (m, 0, 0), (-m, 1, 1)]
    events += [(0, 0, None), (0, 1, None)]
    low_chunk = lax.rem(z + NZ - lax.div(y, 3), NZ)
    high_chunk = lax.rem(z + lax.div(3 - y, 3), NZ)

    def entry_of(k, chunk, rel):
        return idx[ENTRY + k * OWNERS + chunk * NY + lax.rem(y + rel, NY), plane + y * RUN]

    def offer(event):
        off, kv, _ = event
        chunk = lax.rem(z + off + NZ, NZ)
        for p, rel in ((2, 2), (0, 1), (1, 3)):
            for k in range(2):
                rsend[p, chunk, kv, k * BLOCK : (k + 1) * BLOCK, :] = rp[kv, entry_of(k, chunk, rel)]
        for p in (0, 1, 2):
            back_copy(p, chunk, kv).start()

    done = []

    def collect(event):
        off, kv, _ = event
        chunk = lax.rem(z + off + NZ, NZ)
        for p in range(3):
            back_copy(p, chunk, kv).wait_recv()
        slot = 1 if off < 0 else 0
        if (off, 1 - kv) not in done:
            lane = lax.broadcasted_iota(jnp.int32, (1, HD), 1)
            row = lax.broadcasted_iota(jnp.int32, (ROWS, HD), 0)
            for n, rel in enumerate((0, 3, 1, 2)):
                first, second = [
                    idx[RAW + k * OWNERS + chunk * NY + y, plane + lax.rem(y + rel, NY) * RUN]
                    for k in range(2)
                ]
                target = jnp.where(lane < BLOCK, first, second) * BLOCK + (lane & (BLOCK - 1))
                pickers[slot, :, n * HD : (n + 1) * HD] = jnp.where(
                    row == target, 1.0, 0.0
                ).astype(jnp.bfloat16)
        done.append((off, kv))
        data = [rp[kv, entry_of(k, chunk, 0)] for k in range(2)]
        data += [ybuf[p, chunk, kv] for p in range(3)]
        acc[kv] = dot(pickers[slot], jnp.concatenate(data, axis=0), NN)

        @pl.when(chunk == low_chunk)
        def _():
            halo_back(1, kv).wait_recv()
            acc[kv, (RUN - 1) * BLOCK :, :] += hbuf[1, kv].astype(jnp.float32)

        @pl.when(chunk == high_chunk)
        def _():
            halo_back(0, kv).wait_recv()
            acc[kv, :BLOCK, :] += hbuf[0, kv].astype(jnp.float32)

        @pl.when(jnp.logical_and(chunk == 0, y == 0))
        def _():
            total = glob[kv].astype(jnp.float32)
            for m in range(3):
                global_back(m, kv).wait_recv()
                total = total + gbuf[m, kv].astype(jnp.float32)
            acc[kv, 0 : 2 * BLOCK, :] += total

    bufs = (zup, zdown)
    zpeer = (zu, zd)

    def zring(i, t, kv, n):
        at = pl.ds(n * HALF, HALF) if t < 3 else token_rows(n)
        return send(
            bufs[i].at[0, t, kv, at], bufs[i].at[1, t, kv, at], zs2.at[i, t, kv, n],
            zr2.at[i, t, kv, n], "seq", zpeer[i],
        )

    def zpush(event):
        off, kv, i = event
        t = 4 - abs(off)
        for half in range(2):
            at = pl.ds(half * HALF, HALF)
            total = acc[kv, at, :]
            if t >= 2 or (t == 1 and kv == i):
                zring(i, t - 1, kv, half).wait_recv()
                total = total + bufs[i][1, t - 1, kv, at, :].astype(jnp.float32)
            bufs[i][0, t, kv, at, :] = total.astype(jnp.bfloat16)
            if t < 3:
                zring(i, t, kv, half).start()
        if t == 3:
            for d in (2, 1, 3, 0):
                zring(i, t, kv, d).start()

    def token_rows(d):
        return rows_of(lax.rem(x + d, NX) * 2 * BLOCK, 2 * BLOCK)

    def query_part(n):
        d = (2, 1, 3, 0)[n // 2]
        a = dq_ref[token_rows(d), :]

        def tile(m, carry):
            w = pl.ds(pl.multiple_of(m * TILE, TILE), TILE)
            total_ref[d, :, w] = dot(a, wq[w, :], NT)
            return carry

        half = D // TILE // 2
        lax.fori_loop(n % 2 * half, n % 2 * half + half, tile, 0)

    ahead = 5
    for n, event in enumerate(events[:ahead]):
        if n < 2:
            for m in range(1, NY):
                @pl.when(y == m)
                def _():
                    global_back(m - 1, n).start()
        offer(event)
    for p in range(2):
        for kv in range(2):
            halo_back(p, kv).start()
    for load in loads[2:]:
        load.wait()
    query_part(0)
    query_part(1)

    parts = 2
    for n, event in enumerate(events[:14]):
        collect(event)
        zpush(event)
        if n + ahead < 16:
            offer(events[n + ahead])
        if n % 2 == 1 and parts < 8:
            query_part(parts)
            parts += 1
    for kv in range(2):
        collect(events[14 + kv])

    def settle(d):
        at = token_rows(d)
        shifted = rows_of(lax.rem(x + d, NX) * 2 * BLOCK + BLOCK, 2 * BLOCK)
        for kv in range(2):
            total = acc[kv, at, :] + wacc[kv, shifted, :]
            for i in range(2):
                zring(i, 3, kv, d).wait_recv()
                total = total + bufs[i][1, 3, kv, at, :].astype(jnp.float32)
            dkv[at, kv * HD : (kv + 1) * HD] = total.astype(jnp.bfloat16)

    def cols(quarter):
        return pl.ds(quarter * QUARTER, QUARTER)

    def pair_copy(d, quarter):
        return send(
            term.at[d, rows_of((1 - c) * BLOCK, BLOCK), cols(quarter)],
            pair.at[d, :, cols(quarter)], ps.at[d, quarter], pr.at[d, quarter],
            "head", partner,
        )

    def xring(i, t, quarter):
        return send(
            xout.at[i, t, :, cols(quarter)], xin.at[i, t, :, cols(quarter)],
            xs.at[i, t, quarter], xr.at[i, t, quarter], "head", xpeers[i],
        )

    def compute(d):
        settle(d)
        a = dkv[token_rows(d), :]
        for quarter in range(4):
            def tile(n, carry):
                w = pl.ds(pl.multiple_of(quarter * QUARTER + n * TILE, TILE), TILE)
                total = total_ref[d, :, w] + dot(a, wkv[w, :], NT)
                term[d, :, w] = total.astype(jnp.bfloat16)
                return carry

            lax.fori_loop(0, QUARTER // TILE, tile, 0)
            pair_copy(d, quarter).start()

    def both(d, quarter):
        pair_copy(d, quarter).wait_recv()
        mine = term[d, rows_of(c * BLOCK, BLOCK), cols(quarter)].astype(jnp.float32)
        return mine + pair[d, :, cols(quarter)].astype(jnp.float32)

    def arrived(i, t, quarter):
        xring(i, t, quarter).wait_recv()
        return xin[i, t, :, cols(quarter)].astype(jnp.float32)

    def xpush(i, t, quarter, total):
        xout[i, t, :, cols(quarter)] = total.astype(jnp.bfloat16)
        xring(i, t, quarter).start()

    compute(2)
    compute(1)
    for n in range(2):
        xpush(0, 0, n, both(2, n))
        xpush(1, 0, 2 + n, both(2, 2 + n))
    compute(3)
    for n in range(2):
        xpush(0, 1, 2 + n, both(1, 2 + n))
        xpush(1, 1, n, both(3, n))
    compute(0)
    for n in range(2):
        xpush(0, 1, n, both(1, n) + arrived(0, 0, n))
        xpush(1, 1, 2 + n, both(3, 2 + n) + arrived(1, 0, 2 + n))
    for quarter in (2, 3, 0, 1):
        total = both(0, quarter) + arrived(0, 1, quarter) + arrived(1, 1, quarter)
        out[:, cols(quarter)] = total.astype(jnp.bfloat16)

    for i in range(2):
        for t in range(4):
            for kv in range(2):
                for half in range(2):
                    if t < 3 or kv == i:
                        ring(i == 0, t, kv, half).wait_send()
                for n in range(2 if t < 3 else 4):
                    if t > 0 or kv == i:
                        zring(i, t, kv, n).wait_send()
    for p in range(3):
        for n in range(NZ):
            for kv in range(2):
                slot_copy(p, n, kv).wait_send()
                back_copy(p, n, kv).wait_send()
    for p in range(2):
        for kv in range(2):
            halo_copy(p, kv).wait_send()
            halo_back(p, kv).wait_send()

    @pl.when(y == 0)
    def _():
        for p in range(3):
            for kv in range(2):
                global_copy(p, kv).wait_send()

    @pl.when(y != 0)
    def _():
        for kv in range(2):
            global_back(0, kv).wait_send()

    for d in range(4):
        for quarter in range(4):
            pair_copy(d, quarter).wait_send()
    for i in range(2):
        for quarter in range(4):
            if quarter // 2 == i:
                xring(i, 0, quarter).wait_send()
            xring(i, 1, quarter).wait_send()


def whole(owners, blocks, keys, values, query, grad_out, wq, wk, wv):
    anywhere = pl.BlockSpec(memory_space=pltpu.HBM)
    half = jnp.bfloat16
    full = jnp.float32
    slots = (3, NZ, 2, 2 * BLOCK, HD)
    return pl.pallas_call(
        whole_kernel,
        out_shape=sds((BLOCK, D)),
        in_specs=[anywhere] * 9,
        out_specs=vmem(),
        scratch_shapes=[
            VM((3, OWNERS * RUN), jnp.int32),
            VM((3, OWNERS * RUN), jnp.int32),
            VM((LISTS + 8, 128), jnp.int32),
            pltpu.SMEM((LISTS + 8, 128), jnp.int32),
            VM((2, TABLE * BLOCK, HD), half),
            VM((2, RUN, BLOCK, HD), half),
            VM(slots, half),
            VM((ROWS, GROUP * HD), half),
            VM((ROWS, GROUP * HD), half),
            VM((ROWS, GROUP * HD), half),
            VM((PER, ROWS, HD), half),
            VM((PER, ROWS, HD), half),
            VM((2, ROWS + 2 * BLOCK, HD), full),
            VM((2, 2 * BLOCK, HD), full),
            VM((2, RUN * 3, BLOCK, HD), half),
            VM((2, 2 * BLOCK, HD), half),
            VM((2, 2 * BLOCK, HD), half),
            VM((D, GROUP * HD), half),
            VM((D, 2 * HD), half),
            VM((ROWS, 2 * HD), half),
            VM(slots, half),
            VM(slots, half),
            VM((2, 2, BLOCK, HD), half),
            VM((3, 2, 2 * BLOCK, HD), half),
            VM((2, ROWS, ROWS), half),
            VM((2, ROWS, HD), full),
            VM((2, 4, 2, ROWS, HD), half),
            VM((2, 4, 2, ROWS, HD), half),
            VM((4, 2 * BLOCK, D), full),
            VM((4, 2 * BLOCK, D), half),
            VM((4, BLOCK, D), half),
            VM((2, 2, BLOCK, D), half),
            VM((2, 2, BLOCK, D), half),
            DMA,
            DMA((9,)),
            DMA((2, 4, 4)),
            DMA((2, 4, 4)),
            DMA((3, NZ, 2)),
            DMA((3, NZ, 2)),
            DMA((2, 2)),
            DMA((2, 2)),
            DMA((3, 2)),
            DMA((2,)),
            DMA((2, 4, 2, 4)),
            DMA((2, 4, 2, 4)),
            DMA((3, NZ, 2)),
            DMA((3, NZ, 2)),
            DMA((2, 2)),
            DMA((2, 2)),
            DMA((2,)),
            DMA((3, 2)),
            DMA((4, 4)),
            DMA((4, 4)),
            DMA((2, 2, 4)),
            DMA((2, 2, 4)),
        ],
        compiler_params=pltpu.CompilerParams(
            collective_id=0, has_side_effects=True, vmem_limit_bytes=60 * 2**20
        ),
        name="whole",
    )(owners, blocks, keys, values, query, grad_out, wq, wk, wv)


def on_device(query, keys, values, grad_out, w_query, w_key, w_value, rand_owner, rand_block):
    return whole(
        rand_owner.T, rand_block.T, keys, values, query, grad_out, w_query, w_key, w_value
    )


def solution(mesh):
    return jax.shard_map(
        on_device,
        mesh=mesh,
        in_specs=(
            P("seq", "head"),
            P("seq", "head"),
            P("seq", "head"),
            P("seq", "head"),
            P(None, "head"),
            P(None, "head"),
            P(None, "head"),
            P(),
            P(),
        ),
        out_specs=P(("seq", "head"), None),
        check_vma=False,
    )
```
